512 devices in a mesh: frag: 16 (over y, x_hi, core), band: 32 (over z, x_lo).
Axes of the slice: x: 4 (x_hi: 2, x_lo: 2; x = x_hi * 2 + x_lo), y: 4, z: 16, core: 2. Of those that a mesh axis runs over, the one named last changes fastest.
Arguments:
- bands_in: bfloat16 [16, 128, 32768], P('frag', 'band'), may hold values from -13 to 13
- potential_in: float32 [16, 64, 4096], P('frag', 'band'), may hold values from -6 to 6
- hartree: float32 [64, 128, 128], P('band', 'frag'), may hold values from -6 to 6
- patch_list: int32 [16, 3], replicated, may hold values from -1 to 127, as said below
Outputs:
- bands_out: float32 [16, 128, 32768], P('frag', 'band')
- potential_out: float32 [16, 64, 4096], P('frag', 'band')
The draws below stay inside these ranges and needn't reach their ends.
Inputs may be any that keep to these rules, and one draw needn't show every extreme that they name: `patch_list`: column 0 is -1 or +1 and both occur; columns 1 and 2 run from 0 to 127 and the largest offset occurs.
All inputs are finite; a program needn't handle non-finite values.
Results may differ from the reference program's by a relative error of at most 0.0043.
Values may be sent and summed in bfloat16 or wider, within the bound.
No kernel may reach another device: no remote copies, remote signals or barrier semaphores. Data moves between devices by JAX's collectives and lax.ppermute only.
A program may use at most 64 MiB of HBM per device.

```python
import math
import jax
import jax.numpy as jnp
from jax import lax

FG = 64
NB = 128
NEWTON = 6
COEF = 16384
FRAGS = 16
GY = 128
GZ = 128


def draw_bands_in(key, part):
    base = jax.random.fold_in(key, 11)
    keys = jax.random.split(base, 1)
    raw = jnp.clip(jax.random.normal(keys[0], (FRAGS, NB, 2 * COEF), jnp.float32), -6.0, 6.0)
    values = raw + 0.5 * jnp.roll(raw, 1, axis=1)
    return values.astype(jnp.bfloat16)


def draw_patch_list(key, part):
    base = jax.random.fold_in(key, 23)
    keys = jax.random.split(base, 6)
    places = jnp.arange(FRAGS)
    signs = jnp.where(jax.random.randint(keys[0], (FRAGS,), 0, 2) == 0, -1, 1)
    first_pick = jax.random.randint(keys[1], (), 0, FRAGS)
    second_pick = (first_pick + 1 + jax.random.randint(keys[2], (), 0, FRAGS - 1)) % FRAGS
    signs = jnp.where(places == first_pick, -1, jnp.where(places == second_pick, 1, signs))
    offset_y = jax.random.randint(keys[3], (FRAGS,), 0, 2 * FG)
    offset_z = jax.random.randint(keys[4], (FRAGS,), 0, 2 * FG)
    top_pick = jax.random.randint(keys[5], (), 0, FRAGS)
    offset_y = jnp.where(places == top_pick, 2 * FG - 1, offset_y)
    return jnp.stack([signs, offset_y, offset_z], axis=1).astype(jnp.int32)


def block_levels(rng, shape, cuts, smallest, largest):
    def one(axis_at, blocks):
        draws = jax.random.uniform(jax.random.fold_in(jax.random.fold_in(rng, 6), axis_at), (blocks,), jnp.float32, smallest / len(cuts), largest / len(cuts))
        return jnp.repeat(jnp.exp(draws), shape[axis_at] // blocks).reshape((-1,) + (1,) * (len(shape) - axis_at - 1))

    level = one(*cuts[0])
    for cut in cuts[1:]:
        level = level * one(*cut)
    return level


def noise(stream_key, dims, scale, reach, cuts=(), held_as=jnp.bfloat16):
    level = block_levels(stream_key, dims, cuts, -0.22, 0.18) if cuts else 1.0
    drawn = jax.random.normal(stream_key, dims, jnp.float32) * scale * level
    return jnp.minimum(jnp.maximum(drawn, -reach), reach).astype(held_as)


def setup_inputs(seed: int = 0) -> dict:
    splits = jax.random.split(jax.random.key(seed), 5)
    return {
        "bands_in": draw_bands_in(jax.random.fold_in(splits[4], 71), 0),
        "potential_in": noise(splits[1], (FRAGS, FG, FG * FG), 1.0, 6.0, ((0, 16), (1, 32)), jnp.float32),
        "hartree": noise(splits[2], (FG, GY, GZ), 1.0, 6.0, ((0, 32), (1, 16)), jnp.float32),
        "patch_list": draw_patch_list(jax.random.fold_in(splits[4], 71), 0),
    }


SLATER = 0.9847
SOFTEN = 0.25
STEP_TAU = 0.5
NORM_EPS = 1e-06

def dft_tables(grid_n):
    half_box = grid_n // 2
    quart_box = grid_n // 4
    places = jnp.arange(grid_n, dtype=jnp.float32)
    freq_xy = jnp.arange(half_box, dtype=jnp.float32) - half_box // 2
    freq_z = jnp.arange(quart_box, dtype=jnp.float32) - quart_box // 2
    angle_xy = 2.0 * math.pi / grid_n * places[:, None] * freq_xy[None, :]
    angle_z = 2.0 * math.pi / grid_n * freq_z[:, None] * places[None, :]
    cos_xy = jnp.cos(angle_xy)
    sin_xy = jnp.sin(angle_xy)
    cos_z = jnp.cos(angle_z)
    sin_z = jnp.sin(angle_z)
    fwd_xy = jnp.concatenate([cos_xy, sin_xy], axis=1)
    back_xy = jnp.concatenate([cos_xy.T, -sin_xy.T], axis=1)
    fwd_z = jnp.concatenate([jnp.concatenate([cos_z, sin_z], axis=1), jnp.concatenate([-sin_z, cos_z], axis=1)], axis=0)
    back_z = jnp.concatenate([jnp.concatenate([cos_z.T, -sin_z.T], axis=1), jnp.concatenate([sin_z.T, cos_z.T], axis=1)], axis=0)
    return (fwd_z.astype(jnp.bfloat16), fwd_xy.astype(jnp.bfloat16), back_xy.astype(jnp.bfloat16), back_z.astype(jnp.bfloat16))

def kinetic(grid_n):
    half_box = grid_n // 2
    quart_box = grid_n // 4
    freq_xy = jnp.arange(half_box, dtype=jnp.float32) - half_box // 2
    freq_z = jnp.arange(quart_box, dtype=jnp.float32) - quart_box // 2
    squares = freq_xy[:, None, None, None] ** 2 + freq_xy[None, :, None, None] ** 2 + freq_z[None, None, None, :] ** 2
    squares = jnp.broadcast_to(squares, (half_box, half_box, 2, quart_box))
    return (16.0 * squares / (grid_n * grid_n)).reshape(-1)

def swap_parts(values, half_n):
    return jnp.concatenate([-values[..., half_n:], values[..., :half_n]], axis=-1)

def to_grid(band_row, tables, grid_n):
    fwd_z, fwd_xy, back_xy, back_z = tables
    half_box = grid_n // 2
    quart_box = grid_n // 4
    section_out = jnp.dot(band_row.reshape(half_box * half_box, 2 * quart_box), fwd_z, preferred_element_type=jnp.float32)
    section_out = section_out.astype(jnp.bfloat16).reshape(half_box, half_box, 2 * grid_n)
    stacked = jnp.concatenate([section_out, swap_parts(section_out, grid_n)], axis=1)
    section_out = jnp.einsum('yj,xjc->xyc', fwd_xy.astype(jnp.float32), stacked.astype(jnp.float32)).astype(jnp.bfloat16)
    stacked = jnp.concatenate([section_out, swap_parts(section_out, grid_n)], axis=0).reshape(2 * half_box, 2 * grid_n * grid_n)
    grid_vals = jnp.dot(fwd_xy, stacked, preferred_element_type=jnp.float32) * (4.0 / grid_n ** 1.5)
    return grid_vals.reshape(grid_n, grid_n, 2 * grid_n)

def to_box(field, tables, grid_n):
    fwd_z, fwd_xy, back_xy, back_z = tables
    half_box = grid_n // 2
    stacked = jnp.concatenate([field, swap_parts(field, grid_n)], axis=0).reshape(2 * grid_n, 2 * grid_n * grid_n)
    section_out = jnp.dot(back_xy, stacked, preferred_element_type=jnp.float32)
    section_out = section_out.astype(jnp.bfloat16).reshape(half_box, grid_n, 2 * grid_n)
    stacked = jnp.concatenate([section_out, swap_parts(section_out, grid_n)], axis=1)
    section_out = jnp.einsum('yj,xjc->xyc', back_xy.astype(jnp.float32), stacked.astype(jnp.float32)).astype(jnp.bfloat16)
    box_vals = jnp.dot(section_out.reshape(half_box * half_box, 2 * grid_n), back_z, preferred_element_type=jnp.float32)
    return (box_vals * (0.25 / grid_n ** 1.5)).reshape(-1)

def step_band(band_row, potential, tables, kinetic_diag, grid_n):
    grid_vals = to_grid(band_row, tables, grid_n)
    weighted = (grid_vals.reshape(grid_n, grid_n, 2, grid_n) * potential[:, :, None, :]).reshape(grid_n, grid_n, 2 * grid_n)
    image = to_box(weighted.astype(jnp.bfloat16), tables, grid_n)
    widened = band_row.astype(jnp.float32)
    return (widened - STEP_TAU * (kinetic_diag * widened + image)).astype(jnp.bfloat16)

def conj_parts(band_rows, quart_box):
    rows_n, width_n = band_rows.shape
    blocks = band_rows.reshape(rows_n, width_n // (2 * quart_box), 2, quart_box)
    return jnp.stack([blocks[:, :, 1], -blocks[:, :, 0]], axis=2).reshape(rows_n, width_n)

def real_dot(left_mat, right_mat):
    return jnp.dot(left_mat, right_mat, precision=lax.Precision.HIGHEST, preferred_element_type=jnp.float32)

def complex_mul(left_pair, right_pair):
    return (real_dot(left_pair[0], right_pair[0]) - real_dot(left_pair[1], right_pair[1]), real_dot(left_pair[0], right_pair[1]) + real_dot(left_pair[1], right_pair[0]))

def newton(gram_re, gram_im, steps_n):
    size_n = gram_re.shape[0]
    scale = jnp.sqrt(jnp.sum(gram_re * gram_re + gram_im * gram_im) + NORM_EPS)
    identity = jnp.eye(size_n, dtype=jnp.float32)
    iter_y = (gram_re / scale, gram_im / scale)
    iter_z = (identity, jnp.zeros_like(identity))
    for newton_step in range(steps_n):
        product = complex_mul(iter_z, iter_y)
        factor = (1.5 * identity - 0.5 * product[0], -0.5 * product[1])
        iter_y = complex_mul(iter_y, factor)
        iter_z = complex_mul(factor, iter_z)
    root = jnp.sqrt(scale)
    return (iter_z[0] / root, iter_z[1] / root)

def band_density(band_rows, tables, grid_n):

    def add_band(carry, band_row):
        grid_vals = to_grid(band_row, tables, grid_n)
        return (carry + grid_vals * grid_vals, None)
    summed, unused = lax.scan(add_band, jnp.zeros((grid_n, grid_n, 2 * grid_n), jnp.float32), band_rows)
    return summed.reshape(grid_n, grid_n, 2, grid_n).sum(axis=2)

def xc_potential(values):
    return -SLATER * values / jnp.power(values * values + SOFTEN, 1.0 / 3.0)

def contract_first(left_mat, right_mat):
    return lax.dot_general(left_mat, right_mat.astype(jnp.float32), (((0,), (0,)), ((), ())), precision=lax.Precision.HIGHEST, preferred_element_type=jnp.float32)

def contract_last(left_mat, right_mat):
    return lax.dot_general(left_mat, right_mat, (((1,), (1,)), ((), ())), preferred_element_type=jnp.float32)

def reference(bands_in, potential_in, hartree, patch_list):
    tables = dft_tables(FG)
    kinetic_diag = kinetic(FG)

    def fragment(packed):
        band_rows, flat_pot = packed
        potential = flat_pot.reshape(FG, FG, FG)

        def step_one(band_row):
            return step_band(band_row, potential, tables, kinetic_diag, FG)
        stepped = lax.map(step_one, band_rows)
        swapped = conj_parts(stepped, FG // 4)
        gram_re = contract_last(stepped, stepped) / COEF
        gram_im = contract_last(stepped, swapped) / COEF
        inv_re, inv_im = newton(gram_re, gram_im, NEWTON)
        new_rows = contract_first(inv_re, stepped) - contract_first(inv_im, swapped)
        density = band_density(new_rows, tables, FG) * (2.0 / NB)
        return (new_rows, density)
    bands_out, densities = lax.map(fragment, (bands_in, potential_in))

    def place(carry, packed):
        density, entry = packed
        placed = jnp.pad(density, ((0, 0), (0, GY - FG), (0, GZ - FG)))
        moved = jnp.roll(placed, (entry[1], entry[2]), axis=(1, 2))
        return (carry + entry[0].astype(jnp.float32) * moved, None)
    patched, unused = lax.scan(place, jnp.zeros((FG, GY, GZ), jnp.float32), (densities, patch_list))
    total = hartree + xc_potential(patched)

    def extract(entry):
        moved = jnp.roll(total, (-entry[1], -entry[2]), axis=(1, 2))
        return moved[:, :FG, :FG].reshape(FG, FG * FG)
    potential_out = lax.map(extract, patch_list)
    return (bands_out, potential_out)
```

```python
import math

import numpy as np

import jax
import jax.numpy as jnp
from jax import lax
from jax.experimental import pallas as pl
from jax.experimental.pallas import tpu as pltpu
from jax.sharding import PartitionSpec as P

FG = 64
NB = 128
NEWTON = 6
COEF = 16384
FRAGS = 16
GY = 128
GZ = 128
HB = FG // 2
QB = FG // 4

SLATER = 0.9847
SOFTEN = 0.25
STEP_TAU = 0.5
NORM_EPS = 1e-06

F32 = jnp.float32
BF16 = jnp.bfloat16
LOCAL = 4
LANES = 128


def dft_tables():
    places = np.arange(FG)
    freq_xy = np.arange(HB) - HB // 2
    freq_z = np.arange(QB) - QB // 2
    turn_xy = 2.0 * math.pi / FG * ((places[:, None] * freq_xy[None, :]) % FG)
    turn_z = 2.0 * math.pi / FG * ((freq_z[:, None] * places[None, :]) % FG)
    cos_xy, sin_xy = np.cos(turn_xy), np.sin(turn_xy)
    cos_z, sin_z = np.cos(turn_z), np.sin(turn_z)
    same = np.eye(LOCAL)
    fwd_x = np.stack([np.einsum("ab,xk->axbk", same, t) for t in (cos_xy, sin_xy)], axis=2)
    fwd_x = fwd_x.reshape(LOCAL * FG, 2 * LOCAL * HB)
    fwd_x_send = (
        fwd_x.reshape(LOCAL, FG // 2, 2, -1).transpose(1, 2, 0, 3).reshape(LOCAL * FG, -1)
    )
    back_x = np.stack([np.einsum("ab,xk->akbx", same, t) for t in (cos_xy, -sin_xy)], axis=2)
    back_x = back_x.reshape(LOCAL * HB, 2 * LOCAL * FG)
    fwd_y = np.stack(
        [np.stack([cos_xy.T, sin_xy.T], axis=2), np.stack([-sin_xy.T, cos_xy.T], axis=2)], axis=1
    ).reshape(2 * HB, 2 * FG)
    one_z = np.block([[cos_z, sin_z], [-sin_z, cos_z]])
    fwd_z = np.einsum("ab,kz->akbz", same, one_z).reshape(LOCAL * 2 * QB, LOCAL * 2 * FG)
    send = np.einsum("ab,kl->kabl", same, np.eye(HB)).reshape(LOCAL * HB, LOCAL * HB)
    return tuple(
        jnp.asarray(t, dtype=F32).astype(BF16)
        for t in (fwd_x, fwd_x_send, back_x, fwd_y, fwd_z, send)
    )


def iota(shape, axis):
    return lax.broadcasted_iota(jnp.int32, shape, axis)


def dot(left, right):
    return jnp.dot(left, right, preferred_element_type=F32)


def dot_t(left, right):
    return lax.dot_general(left, right, (((1,), (1,)), ((), ())), preferred_element_type=F32)


def times_i(block):
    first = iota(block.shape, 1) % (2 * QB) < QB
    ahead = pltpu.roll(block, LANES - QB, 1)
    behind = pltpu.roll(block, QB, 1)
    return jnp.where(first, -ahead, behind)


def halves(values):
    upper = values.astype(BF16)
    return upper, (values - upper.astype(F32)).astype(BF16)


def forward_kernel(bands_ref, fwd_x_ref, fwd_y_ref, big_y_ref, out_ref, rows_ref, stack_ref):
    width = FG * 2 * QB
    spread = (iota((2 * FG, width), 1) // QB == iota((2 * FG, width), 0)).astype(F32).astype(BF16)
    rows_ref[...] = dot(fwd_y_ref[...], spread)
    same = iota((QB, width), 1) % QB == iota((QB, width), 0)

    @pl.loop(0, 2 * HB)
    def _(row):
        line = jnp.broadcast_to(rows_ref[pl.ds(row, 1), :], (QB, width))
        start = pl.multiple_of(row * QB, QB)
        big_y_ref[pl.ds(start, QB), :] = jnp.where(same, line, 0.0).astype(BF16)

    rows_n = LOCAL * HB
    stack_ref[:rows_n, :] = bands_ref[...]
    for start in range(0, HB * 2 * QB, LANES):
        block = bands_ref[:, start : start + LANES].astype(F32)
        stack_ref[rows_n:, start : start + LANES] = times_i(block).astype(BF16)
    after_x = dot(fwd_x_ref[...], stack_ref[...]).astype(BF16)

    @pl.loop(0, width // 512)
    def _(at):
        span = pl.ds(pl.multiple_of(at * 512, 512), 512)
        out_ref[:, span] = dot(after_x, big_y_ref[:, span]).astype(BF16)


def spread_parts(pair):
    low = iota(pair.shape, 1) < FG
    turned = pltpu.roll(pair, FG, 1)
    return jnp.where(low, pair, turned), jnp.where(low, turned, pair)


def step_kernel(
    after_y_ref, pot_ref, bands_ref, big_y_ref, fwd_z_ref, back_x_ref, fwd_x_ref, send_ref,
    stepped_ref, image_ref, back_ref, stack_ref, stack2_ref,
):
    fwd_z = fwd_z_ref[...]

    @pl.loop(0, FG // LOCAL)
    def _(at):
        span = pl.ds(pl.multiple_of(at * LANES, LANES), LANES)
        grid_vals = dot(after_y_ref[:, span], fwd_z) * (4.0 / FG**1.5)
        pot = pot_ref[:, pl.ds(pl.multiple_of(at * 2 * LANES, 2 * LANES), 2 * LANES)].astype(F32)
        pots = jnp.concatenate(
            [*spread_parts(pot[:, :LANES]), *spread_parts(pot[:, LANES:])], axis=1
        )
        pots = jnp.concatenate([pots] * LOCAL, axis=0)
        weighted = (grid_vals * pots).astype(BF16)
        back_ref[:, span] = dot_t(weighted, fwd_z).astype(BF16)

    rows_n = LOCAL * FG

    @pl.loop(0, HB * 2 * QB // LANES)
    def _(at):
        span = pl.ds(pl.multiple_of(at * LANES, LANES), LANES)
        block = dot_t(back_ref[...], big_y_ref[span, :])
        stack_ref[:rows_n, span] = block.astype(BF16)
        stack_ref[rows_n:, span] = times_i(block).astype(BF16)

    half_n = LOCAL * HB
    for start in range(0, HB * 2 * QB, LANES):
        image = dot(back_x_ref[...], stack_ref[:, start : start + LANES]) * (0.25 / FG**1.5)
        shape = (half_n, LANES)
        row, lane = iota(shape, 0), iota(shape, 1) + start
        mx, my = row % HB - HB // 2, lane // (2 * QB) - HB // 2
        mz = lane % QB - QB // 2
        kinetic = (mx * mx + my * my + mz * mz).astype(F32) * (16.0 / FG**2)
        wide = bands_ref[:, start : start + LANES].astype(F32)
        stepped = (wide - STEP_TAU * (kinetic * wide + image)).astype(BF16)
        stack2_ref[:half_n, start : start + LANES] = stepped
        stack2_ref[half_n:, start : start + LANES] = times_i(stepped.astype(F32)).astype(BF16)
    stepped_ref[...] = dot(send_ref[...], stack2_ref[:half_n, :]).astype(BF16)
    image_ref[...] = dot(fwd_x_ref[...], stack2_ref[...]).astype(BF16)


def gram_kernel(stepped_ref, out_ref, conj_ref):
    for start in range(0, HB * 2 * QB, LANES):
        block = stepped_ref[:, start : start + LANES].astype(F32)
        conj_ref[:, start : start + LANES] = (-times_i(block)).astype(BF16)
    stepped = stepped_ref[...]
    gram_re = dot_t(stepped, stepped)
    gram_im = dot_t(stepped, conj_ref[...])
    shape = (NB, NB)
    out_ref[...] = jnp.where(iota(shape, 0) >= iota(shape, 1), gram_re, gram_im) * (1.0 / COEF)


def complex_mul(left, right):
    turned = jnp.concatenate([-left[NB:], left[:NB]], axis=0)
    left_hi, left_lo = halves(jnp.concatenate([left, turned], axis=1))
    right_hi, right_lo = halves(right)
    first = dot(left_hi, jnp.concatenate([right_hi, right_lo], axis=1))
    return first[:, :NB] + (first[:, NB:] + dot(left_lo, right_hi))


def newton_kernel(gram_ref, stepped_ref, phi_ref, inv_ref, stack_ref):
    packed = gram_ref[...]
    flipped = packed.T
    shape = (NB, NB)
    row, col = iota(shape, 0), iota(shape, 1)
    gram_re = jnp.where(row >= col, packed, flipped)
    gram_im = jnp.where(row < col, packed, jnp.where(row > col, -flipped, 0.0))
    total = jnp.sum(gram_re * gram_re + gram_im * gram_im, axis=1, keepdims=True)
    scale = jnp.sqrt(jnp.sum(total, axis=0, keepdims=True) + NORM_EPS)
    eye = (row == col).astype(F32)
    identity = jnp.concatenate([eye, jnp.zeros(shape, F32)], axis=0)
    iter_y = jnp.concatenate([gram_re, gram_im], axis=0) / scale
    iter_z = identity
    for at in range(NEWTON):
        product = complex_mul(iter_z, iter_y) if at else iter_y
        factor = 1.5 * identity - 0.5 * product
        if at < NEWTON - 1:
            iter_y = complex_mul(iter_y, factor)
        iter_z = complex_mul(factor, iter_z) if at else factor
    inverse = iter_z / jnp.sqrt(scale)
    inv_re, inv_im = inverse[:NB].T, inverse[NB:].T
    re_hi, re_lo = halves(inv_re)
    im_hi, im_lo = halves(inv_im)
    inv_ref[...] = jnp.concatenate([re_hi, im_hi, re_lo, im_lo], axis=0)
    stack_ref[:NB, :] = stepped_ref[...]
    for start in range(0, HB * 2 * QB, LANES):
        block = stepped_ref[:, start : start + LANES].astype(F32)
        stack_ref[NB:, start : start + LANES] = times_i(block).astype(BF16)
    left = jnp.concatenate(
        [jnp.concatenate([re_hi, im_hi], axis=1), jnp.concatenate([re_lo, im_lo], axis=1)], axis=0
    )
    both = dot(left, stack_ref[...])
    phi_ref[...] = (both[:NB] + both[NB:]).astype(BF16)


def density_kernel(
    place_ref, own_ref, image_ref, inv_ref, big_y_ref, fwd_z_ref,
    out_ref, stack_ref, phi_ref, after_y_ref, dens_ref, wide_ref,
):
    rows_n = 2 * NB
    shape = (NB, 2 * rows_n)
    row, col = iota(shape, 0), iota(shape, 1)
    inner = col % rows_n
    picks = (inner // 8 * LOCAL + inner % LOCAL == row) & (inner // LOCAL % 2 == col // rows_n)
    spread = dot(inv_ref[...], picks.astype(F32).astype(BF16)).astype(BF16)
    stack_ref[:rows_n, :] = image_ref[...]
    for start in range(0, HB * 2 * QB, LANES):
        block = image_ref[:, start : start + LANES].astype(F32)
        stack_ref[rows_n:, start : start + LANES] = times_i(block).astype(BF16)
    left = jnp.concatenate(
        [
            jnp.concatenate(
                [
                    spread[base : base + NB, at * rows_n : (at + 1) * rows_n]
                    for base in (low, low + NB)
                ],
                axis=1,
            )
            for low in (0, 2 * NB)
            for at in (0, 1)
        ],
        axis=0,
    )
    both = dot(left, stack_ref[...])
    phi_ref[...] = (both[:rows_n] + both[rows_n:]).astype(BF16)
    width = FG * 2 * QB

    @pl.loop(0, width // 512)
    def _(at):
        span = pl.ds(pl.multiple_of(at * 512, 512), 512)
        after_y_ref[:, span] = dot(phi_ref[...], big_y_ref[:, span]).astype(BF16)

    low = iota((1, LANES), 1) < FG

    @pl.loop(0, FG // LOCAL)
    def _(at):
        span = pl.ds(pl.multiple_of(at * LANES, LANES), LANES)
        grid_vals = dot(after_y_ref[:, span], fwd_z_ref[...]) * (4.0 / FG**1.5)
        square = grid_vals * grid_vals
        sums = [
            jnp.sum(square[plane * NB : (plane + 1) * NB], axis=0, keepdims=True) * (2.0 / NB)
            for plane in (0, 1)
        ]
        for y_lo in range(LOCAL):
            parts = [s[:, y_lo * LANES : (y_lo + 1) * LANES] for s in sums]
            full = [p + pltpu.roll(p, FG, 1) for p in parts]
            dens_ref[pl.ds(at * LOCAL + y_lo, 1), :] = jnp.where(low, full[0], full[1])

    own = own_ref[0]
    own_y, own_z = place_ref[own, 1], place_ref[own, 2]
    sign = place_ref[own, 0].astype(F32)
    dens = (dens_ref[...] * sign).astype(BF16)
    shape = (LANES, LANES)
    row, col = iota(shape, 0), iota(shape, 1)
    same_plane = row // FG == col // FG
    rows_shape = (FG, FG)
    rows_row, rows_col = iota(rows_shape, 0), iota(rows_shape, 1)
    for to in range(FRAGS):
        shift_y = place_ref[to, 1] - own_y + GY
        shift_z = place_ref[to, 2] - own_z + GZ
        cols = same_plane & ((col % FG + shift_z) % GZ == row % FG)
        moved = dot(dens, cols.astype(F32).astype(BF16)).astype(BF16)
        rows = (rows_row + shift_y) % GY == rows_col
        out_ref[to] = dot(rows.astype(F32).astype(BF16), moved).astype(BF16)


def hartree_kernel(place_ref, own_ref, tiles_ref, out_ref):
    own = own_ref[0]
    own_y, own_z = place_ref[own, 1], place_ref[own, 2]
    rows = (iota((FG, GY), 0) + own_y) % GY == iota((FG, GY), 1)
    rows = rows.astype(F32).astype(BF16)
    shape = (GZ, LANES)
    row, col = iota(shape, 0), iota(shape, 1)
    total = jnp.zeros((FG, LANES), F32)
    for plane in (0, 1):
        cols = (col // FG == plane) & ((col % FG + own_z) % GZ == row)
        cols = cols.astype(F32).astype(BF16)
        rest = tiles_ref[:, plane].reshape(GY, GZ)
        for _ in range(3):
            part = rest.astype(BF16)
            total += dot(dot(rows, part).astype(BF16), cols)
            rest = rest - part.astype(F32)
    out_ref[...] = total


def xc_potential(values):
    return -SLATER * values / jnp.power(values * values + SOFTEN, 1.0 / 3.0)


VM = pl.BlockSpec(memory_space=pltpu.VMEM)
SM = pl.BlockSpec(memory_space=pltpu.SMEM)


def sds(shape, dtype):
    return jax.ShapeDtypeStruct(shape, dtype)


def call(kernel, outs, in_specs, scratch, flops, moved, name):
    return pl.pallas_call(
        kernel,
        out_shape=outs,
        in_specs=in_specs,
        out_specs=jax.tree.map(lambda _: VM, outs),
        scratch_shapes=[pltpu.VMEM(s, d) for s, d in scratch],
        cost_estimate=pl.CostEstimate(flops=flops, bytes_accessed=moved, transcendentals=0),
        name=name,
    )


def stages():
    coefs = HB * 2 * QB
    width = FG * 2 * QB
    mega = 1 << 20
    forward = call(
        forward_kernel,
        (sds((coefs, width), BF16), sds((LOCAL * FG, width), BF16)),
        [VM] * 3,
        [((2 * HB, width), F32), ((2 * LOCAL * HB, coefs), BF16)],
        2 * 10**9, 6 * mega, "forward",
    )
    step = call(
        step_kernel,
        (sds((LOCAL * HB, coefs), BF16), sds((LOCAL * FG, coefs), BF16)),
        [VM] * 8,
        [
            ((LOCAL * FG, width), BF16),
            ((2 * LOCAL * FG, coefs), BF16),
            ((2 * LOCAL * HB, coefs), BF16),
        ],
        4 * 10**9, 8 * mega, "step",
    )
    gram = call(
        gram_kernel, sds((NB, NB), F32), [VM], [((NB, coefs), BF16)], 10**8, mega // 2, "gram"
    )
    newton = call(
        newton_kernel,
        (sds((NB, coefs), BF16), sds((4 * NB, NB), BF16)),
        [VM] * 2,
        [((2 * NB, coefs), BF16)],
        10**9, mega, "newton",
    )
    density = call(
        density_kernel,
        sds((FRAGS, FG, LANES), BF16),
        [SM, SM] + [VM] * 4,
        [
            ((4 * NB, coefs), BF16),
            ((2 * NB, coefs), BF16),
            ((2 * NB, width), BF16),
            ((FG, LANES), F32),
            ((8, LANES), F32),
        ],
        4 * 10**9, 6 * mega, "density",
    )
    hartree = call(
        hartree_kernel, sds((FG, LANES), F32), [SM, SM, VM], [], 10**7, mega // 4, "hartree"
    )
    return forward, step, gram, newton, density, hartree


def exchange(values, axis):
    return lax.all_to_all(values, axis, split_axis=0, concat_axis=0, tiled=True)


def per_device(bands_in, potential_in, hartree, patch_list):
    fwd_x, fwd_x_send, back_x, fwd_y, fwd_z, send = dft_tables()
    forward, step, gram, newton, density, hartree_window = stages()
    coefs = HB * 2 * QB
    groups = lax.axis_size("band")
    planes = FG // groups
    own = lax.axis_index("frag").astype(jnp.int32).reshape(1)

    pot_send = jnp.broadcast_to(potential_in.astype(BF16), (groups, planes, FG * FG))
    pot = exchange(pot_send, "band").reshape(FG, FG * FG)
    tiles = exchange(jnp.broadcast_to(hartree[None], (FRAGS, *hartree.shape)), "frag")
    bands = bands_in.reshape(LOCAL * HB, coefs)
    big_y, after_y = forward(bands, fwd_x, fwd_y)
    stepped_send, image_send = step(
        after_y, pot, bands, big_y, fwd_z, back_x, fwd_x_send, send
    )
    stepped = exchange(stepped_send.reshape(groups, LOCAL, coefs), "band").reshape(NB, coefs)
    image = exchange(image_send.reshape(groups, planes * LOCAL, coefs), "band")
    image = image.reshape(2 * NB, coefs)
    window = hartree_window(patch_list, own, tiles)
    part = gram(stepped)
    rows = exchange(part.reshape(groups, LOCAL, NB), "band").sum(axis=0)
    whole = exchange(jnp.broadcast_to(rows[None], (groups, LOCAL, NB)), "band").reshape(NB, NB)
    phi, inverse = newton(whole, stepped)
    phi_local = exchange(phi.reshape(groups, LOCAL, coefs), "band")
    pieces = exchange(density(patch_list, own, image, inverse, big_y, fwd_z), "frag")
    patched = pieces.astype(F32).sum(axis=0)
    total = window + xc_potential(patched)
    back = total.reshape(FG, planes, FG).transpose(1, 0, 2).reshape(1, planes, FG * FG)
    bands_out = phi_local.transpose(1, 0, 2).astype(F32).reshape(1, LOCAL, HB * coefs)
    return (bands_out, back)


def solution(mesh):
    in_specs = (P("frag", "band", None), P("frag", "band", None), P("band", "frag", None), P())
    out_specs = (P("frag", "band", None), P("frag", "band", None))
    return jax.shard_map(
        per_device, mesh=mesh, in_specs=in_specs, out_specs=out_specs, check_vma=False
    )
```

```python
import math

import numpy as np

import jax
import jax.numpy as jnp
from jax import lax
from jax.experimental import pallas as pl
from jax.experimental.pallas import tpu as pltpu
from jax.sharding import PartitionSpec as P


FG = 64
NB = 128
NEWTON = 6
COEF = 16384
FRAGS = 16
GY = 128
GZ = 128
HB = FG // 2
QB = FG // 4

SLATER = 0.9847
SOFTEN = 0.25
STEP_TAU = 0.5
NORM_EPS = 1e-06

F32 = jnp.float32
BF16 = jnp.bfloat16
LOCAL = 4
LANES = 128


def dft_tables():
    places = np.arange(FG)
    freq_xy = np.arange(HB) - HB // 2
    freq_z = np.arange(QB) - QB // 2
    turn_xy = 2.0 * math.pi / FG * ((places[:, None] * freq_xy[None, :]) % FG)
    turn_z = 2.0 * math.pi / FG * ((freq_z[:, None] * places[None, :]) % FG)
    cos_xy, sin_xy = np.cos(turn_xy), np.sin(turn_xy)
    cos_z, sin_z = np.cos(turn_z), np.sin(turn_z)
    same = np.eye(LOCAL)
    fwd_x = np.stack([np.einsum("ab,xk->axbk", same, t) for t in (cos_xy, sin_xy)], axis=2)
    fwd_x = fwd_x.reshape(LOCAL, FG // 4, 2, 2, 2 * LOCAL * HB)
    fwd_x_send = fwd_x.transpose(1, 2, 3, 0, 4).reshape(LOCAL * FG, -1)
    fwd_x = fwd_x.transpose(2, 0, 1, 3, 4).reshape(LOCAL * FG, -1)
    back_x = np.stack([np.einsum("ab,xk->akbx", same, t) for t in (cos_xy, -sin_xy)], axis=2)
    back_x = back_x.reshape(LOCAL * HB, 2, LOCAL, FG // 4, 2, 2).transpose(0, 1, 4, 2, 3, 5)
    back_x = back_x.reshape(LOCAL * HB, 2 * LOCAL * FG)
    fwd_y = np.stack(
        [np.stack([cos_xy.T, sin_xy.T], axis=2), np.stack([-sin_xy.T, cos_xy.T], axis=2)], axis=1
    ).reshape(2 * HB, 2 * FG)
    one_z = np.block([[cos_z, sin_z], [-sin_z, cos_z]])
    fwd_z = np.einsum("ab,kz->akbz", same, one_z).reshape(LOCAL * 2 * QB, LOCAL * 2 * FG)
    send = np.einsum("gh,ab,kl->kgahbl", np.eye(2), same, np.eye(HB))
    send = send.reshape(2 * LOCAL * HB, 2 * LOCAL * HB)
    return tuple(
        jnp.asarray(t, dtype=F32).astype(BF16)
        for t in (fwd_x, fwd_x_send, back_x, fwd_y, fwd_z, send)
    )


def iota(shape, axis):
    return lax.broadcasted_iota(jnp.int32, shape, axis)


def dot(left, right):
    return jnp.dot(left, right, preferred_element_type=F32)


def dot_t(left, right):
    return lax.dot_general(left, right, (((1,), (1,)), ((), ())), preferred_element_type=F32)


def times_i(block):
    first = iota(block.shape, 1) % (2 * QB) < QB
    ahead = pltpu.roll(block, LANES - QB, 1)
    behind = pltpu.roll(block, QB, 1)
    return jnp.where(first, -ahead, behind)


def halves(values):
    upper = values.astype(BF16)
    return upper, (values - upper.astype(F32)).astype(BF16)


def forward_kernel(bands_ref, fwd_x_ref, fwd_y_ref, big_y_ref, out_ref, rows_ref, stack_ref):
    width = FG * 2 * QB
    spread = (iota((2 * FG, width), 1) // QB == iota((2 * FG, width), 0)).astype(F32).astype(BF16)
    rows_ref[...] = dot(fwd_y_ref[...], spread)
    same = iota((QB, width), 1) % QB == iota((QB, width), 0)

    @pl.loop(0, 2 * HB)
    def _(row):
        line = jnp.broadcast_to(rows_ref[pl.ds(row, 1), :], (QB, width))
        start = pl.multiple_of(row * QB, QB)
        big_y_ref[pl.ds(start, QB), :] = jnp.where(same, line, 0.0).astype(BF16)

    rows_n = LOCAL * HB
    stack_ref[:rows_n, :] = bands_ref[...]
    for start in range(0, HB * 2 * QB, LANES):
        block = bands_ref[:, start : start + LANES].astype(F32)
        stack_ref[rows_n:, start : start + LANES] = times_i(block).astype(BF16)
    after_x = dot(fwd_x_ref[...], stack_ref[...]).astype(BF16)

    @pl.loop(0, width // 512)
    def _(at):
        span = pl.ds(pl.multiple_of(at * 512, 512), 512)
        out_ref[:, span] = dot(after_x, big_y_ref[:, span]).astype(BF16)


def spread_parts(pair):
    low = iota(pair.shape, 1) < FG
    turned = pltpu.roll(pair, FG, 1)
    return jnp.where(low, pair, turned), jnp.where(low, turned, pair)


def step_kernel(
    place_ref, after_y_ref, near_ref, far_ref, bands_ref, big_y_ref, fwd_z_ref, back_x_ref, send_ref,
    stepped_ref, sent_ref, back_ref, stack_ref, pots_ref,
):
    fwd_z = fwd_z_ref[...]
    near = place_ref[0]
    quarter = FG * FG // 4
    pick_shape = (FG // 2, 2 * FG)
    for at in range(4):
        pick = (iota(pick_shape, 0) * 4 + at == iota(pick_shape, 1)).astype(F32).astype(BF16)
        span = slice(at * quarter, (at + 1) * quarter)
        pots_ref[near, :, span] = dot(pick, near_ref[...])
        pots_ref[1 - near, :, span] = dot(pick, far_ref[...])

    @pl.loop(0, FG // LOCAL)
    def _(at):
        span = pl.ds(pl.multiple_of(at * LANES, LANES), LANES)
        grid_vals = dot(after_y_ref[:, span], fwd_z) * (4.0 / FG**1.5)
        wide = pl.ds(pl.multiple_of(at * 2 * LANES, 2 * LANES), 2 * LANES)
        pots = []
        for half in (0, 1):
            pot = pots_ref[half, :, wide]
            parts = [*spread_parts(pot[:, :LANES]), *spread_parts(pot[:, LANES:])]
            pots += [jnp.concatenate(parts, axis=1)] * LOCAL
        weighted = (grid_vals * jnp.concatenate(pots, axis=0)).astype(BF16)
        back_ref[:, span] = dot_t(weighted, fwd_z).astype(BF16)

    rows_n = LOCAL * FG
    half_n = LOCAL * HB
    block_n = 2 * LANES

    @pl.loop(0, HB * 2 * QB // block_n)
    def _(at):
        start = pl.multiple_of(at * block_n, block_n)
        span = pl.ds(start, block_n)
        block = dot_t(back_ref[...], big_y_ref[span, :])
        stack_ref[:rows_n, :] = block.astype(BF16)
        for low in (0, LANES):
            turned = times_i(block[:, low : low + LANES])
            stack_ref[rows_n:, low : low + LANES] = turned.astype(BF16)
        image = dot(back_x_ref[...], stack_ref[...]) * (0.25 / FG**1.5)
        shape = (half_n, block_n)
        row, lane = iota(shape, 0), iota(shape, 1) + start
        mx, my = row % HB - HB // 2, lane // (2 * QB) - HB // 2
        mz = lane % QB - QB // 2
        kinetic = (mx * mx + my * my + mz * mz).astype(F32) * (16.0 / FG**2)
        bands = bands_ref[:, span].astype(F32)
        stepped_ref[:, span] = (bands - STEP_TAU * (kinetic * bands + image)).astype(BF16)

    half_w = HB * QB
    halves_of = jnp.concatenate([stepped_ref[:, :half_w], stepped_ref[:, half_w:]], axis=0)
    sent_ref[...] = dot(send_ref[...], halves_of).astype(BF16)


def image_kernel(stepped_ref, fwd_x_ref, image_ref, stack_ref):
    half_n = LOCAL * HB
    stack_ref[:half_n, :] = stepped_ref[...]
    for start in range(0, HB * 2 * QB, LANES):
        block = stepped_ref[:, start : start + LANES].astype(F32)
        stack_ref[half_n:, start : start + LANES] = times_i(block).astype(BF16)
    image_ref[...] = dot(fwd_x_ref[...], stack_ref[...]).astype(BF16)


def onehot(matches):
    return matches.astype(F32).astype(BF16)


def gram_kernel(received_ref, image_ref, out_ref, stepped_ref, conj_ref):
    coefs = HB * 2 * QB
    half_w = coefs // 2
    shape = (NB, 2 * NB)
    row, col = iota(shape, 0), iota(shape, 1)
    at = row // LOCAL * 2 * LOCAL + row % LOCAL
    for half in (0, 1):
        pick = onehot(col == at + half * LOCAL)
        rows = dot(pick, received_ref[...])
        stepped_ref[:, half * half_w : (half + 1) * half_w] = rows.astype(BF16)
        for start in range(0, half_w, LANES):
            block = -times_i(rows[:, start : start + LANES])
            conj_ref[:, half * half_w + start : half * half_w + start + LANES] = block.astype(BF16)
    stepped = stepped_ref[...]
    gram_re = dot_t(stepped, stepped)
    gram_im = dot_t(stepped, conj_ref[...])
    shape = (NB, NB)
    gram = jnp.where(iota(shape, 0) >= iota(shape, 1), gram_re, gram_im) * (1.0 / COEF)
    first, _ = halves(gram)
    second = (gram - first.astype(F32)).astype(BF16)
    third = (gram - first.astype(F32) - second.astype(F32)).astype(BF16)
    shape = (2 * NB, NB)
    row, col = iota(shape, 0), iota(shape, 1)
    at = col // LOCAL * 2 * LOCAL + col % LOCAL
    upper, lower = onehot(row == at), onehot(row == at + LOCAL)
    out_ref[:, :coefs] = image_ref[...]
    out_ref[:, coefs : coefs + NB] = (dot(upper, first) + dot(lower, second)).astype(BF16)
    out_ref[:, coefs + NB :] = dot(upper, third).astype(BF16)


def sum_kernel(parts_ref, out_ref):
    parts = parts_ref[...].astype(F32).reshape(HB, 2 * LOCAL, 2 * NB).sum(axis=0)
    swapped = pltpu.roll(parts, LOCAL, 0)
    whole = (parts + swapped)[:, :NB]
    third = parts[:, NB:] + swapped[:, NB:]
    whole = whole + third
    out_ref[...] = jnp.broadcast_to(whole[None], (NB // 8, 8, NB)).reshape(NB, NB)


def complex_mul(left, right):
    turned = jnp.concatenate([-left[NB:], left[:NB]], axis=0)
    left_hi, left_lo = halves(jnp.concatenate([left, turned], axis=1))
    right_hi, right_lo = halves(right)
    first = dot(left_hi, jnp.concatenate([right_hi, right_lo], axis=1))
    return first[:, :NB] + (first[:, NB:] + dot(left_lo, right_hi))


def newton_kernel(gram_ref, stepped_ref, phi_ref, inv_ref, stack_ref):
    packed = gram_ref[...]
    flipped = packed.T
    shape = (NB, NB)
    row, col = iota(shape, 0), iota(shape, 1)
    gram_re = jnp.where(row >= col, packed, flipped)
    gram_im = jnp.where(row < col, packed, jnp.where(row > col, -flipped, 0.0))
    total = jnp.sum(gram_re * gram_re + gram_im * gram_im, axis=1, keepdims=True)
    scale = jnp.sqrt(jnp.sum(total, axis=0, keepdims=True) + NORM_EPS)
    eye = (row == col).astype(F32)
    identity = jnp.concatenate([eye, jnp.zeros(shape, F32)], axis=0)
    iter_y = jnp.concatenate([gram_re, gram_im], axis=0) / scale
    iter_z = identity
    for at in range(NEWTON):
        product = complex_mul(iter_z, iter_y) if at else iter_y
        factor = 1.5 * identity - 0.5 * product
        if at < NEWTON - 1:
            iter_y = complex_mul(iter_y, factor)
        iter_z = complex_mul(factor, iter_z) if at else factor
    inverse = iter_z / jnp.sqrt(scale)
    inv_re, inv_im = inverse[:NB].T, inverse[NB:].T
    re_hi, re_lo = halves(inv_re)
    im_hi, im_lo = halves(inv_im)
    inv_ref[...] = jnp.concatenate([re_hi, im_hi, re_lo, im_lo], axis=0)
    stack_ref[:NB, :] = stepped_ref[...]
    for start in range(0, HB * 2 * QB, LANES):
        block = stepped_ref[:, start : start + LANES].astype(F32)
        stack_ref[NB:, start : start + LANES] = times_i(block).astype(BF16)
    left = jnp.concatenate(
        [jnp.concatenate([re_hi, im_hi], axis=1), jnp.concatenate([re_lo, im_lo], axis=1)], axis=0
    )
    both = dot(left, stack_ref[...])
    phi_ref[...] = (both[:NB] + both[NB:]).astype(BF16)


def density_kernel(
    place_ref, own_ref, image_ref, inv_ref, big_y_ref, fwd_z_ref, tile_ref,
    out_ref, stack_ref, phi_ref, after_y_ref, dens_ref,
):
    rows_n = 2 * NB
    shape = (NB, 2 * rows_n)
    row, col = iota(shape, 0), iota(shape, 1)
    inner = col % rows_n
    picks = (inner // 8 * LOCAL + inner % LOCAL == row) & (inner // LOCAL % 2 == col // rows_n)
    spread = dot(inv_ref[...], picks.astype(F32).astype(BF16)).astype(BF16)
    stack_ref[:rows_n, :] = image_ref[:, : HB * 2 * QB]
    for start in range(0, HB * 2 * QB, LANES):
        block = image_ref[:, start : start + LANES].astype(F32)
        stack_ref[rows_n:, start : start + LANES] = times_i(block).astype(BF16)
    left = jnp.concatenate(
        [
            jnp.concatenate(
                [
                    spread[base : base + NB, at * rows_n : (at + 1) * rows_n]
                    for base in (low, low + NB)
                ],
                axis=1,
            )
            for low in (0, 2 * NB)
            for at in (0, 1)
        ],
        axis=0,
    )
    both = dot(left, stack_ref[...])
    phi_ref[...] = (both[:rows_n] + both[rows_n:]).astype(BF16)
    width = FG * 2 * QB

    @pl.loop(0, width // 512)
    def _(at):
        span = pl.ds(pl.multiple_of(at * 512, 512), 512)
        after_y_ref[:, span] = dot(phi_ref[...], big_y_ref[:, span]).astype(BF16)

    low = iota((1, LANES), 1) < FG

    @pl.loop(0, FG // LOCAL)
    def _(at):
        span = pl.ds(pl.multiple_of(at * LANES, LANES), LANES)
        grid_vals = dot(after_y_ref[:, span], fwd_z_ref[...]) * (4.0 / FG**1.5)
        square = grid_vals * grid_vals
        sums = [
            jnp.sum(square[plane * NB : (plane + 1) * NB], axis=0, keepdims=True) * (2.0 / NB)
            for plane in (0, 1)
        ]
        for y_lo in range(LOCAL):
            parts = [s[:, y_lo * LANES : (y_lo + 1) * LANES] for s in sums]
            full = [p + pltpu.roll(p, FG, 1) for p in parts]
            dens_ref[pl.ds(at * LOCAL + y_lo, 1), :] = jnp.where(low, full[0], full[1])

    own = own_ref[0]
    own_y, own_z = place_ref[own, 1], place_ref[own, 2]
    sign = place_ref[own, 0].astype(F32)
    dens = (dens_ref[...] * sign).astype(BF16)
    shape = (LANES, LANES)
    row, col = iota(shape, 0), iota(shape, 1)
    same_plane = row // FG == col // FG
    rows_shape = (FG, FG)
    rows_row, rows_col = iota(rows_shape, 0), iota(rows_shape, 1)
    for to in range(FRAGS):
        shift_y = place_ref[to, 1] - own_y + GY
        shift_z = place_ref[to, 2] - own_z + GZ
        cols = same_plane & ((col % FG + shift_z) % GZ == row % FG)
        moved = dot(dens, cols.astype(F32).astype(BF16)).astype(BF16)
        rows = (rows_row + shift_y) % GY == rows_col
        out_ref[to, :FG, :] = dot(rows.astype(F32).astype(BF16), moved).astype(BF16)
        for at, part in enumerate(halves(tile_ref[...].reshape(2 * 8, GZ))):
            out_ref[to, FG + at * 16 : FG + (at + 1) * 16, :] = part


def last_kernel(place_ref, own_ref, pieces_ref, out_ref, total_ref):
    own = own_ref[0]
    own_y, own_z = place_ref[own, 1], place_ref[own, 2]
    patched = jnp.zeros((FG, LANES), F32)
    for at in range(FRAGS):
        patched += pieces_ref[at, :FG, :].astype(F32)
    rows = onehot((iota((FG, GY), 0) + own_y) % GY == iota((FG, GY), 1))
    shape = (GZ, LANES)
    row, col = iota(shape, 0), iota(shape, 1)
    total = jnp.zeros((FG, LANES), F32)
    tiles = pieces_ref[:, FG:, :].astype(F32)
    for plane in (0, 1):
        cols = onehot((col // FG == plane) & ((col % FG + own_z) % GZ == row))
        for part in (0, 1):
            start = part * 16 + plane * 8
            tile = tiles[:, start : start + 8, :].reshape(GY, GZ).astype(BF16)
            total += dot(dot(rows, tile).astype(BF16), cols)
    power = jnp.exp(jnp.log(patched * patched + SOFTEN) * (-1.0 / 3.0))
    total_ref[...] = total - SLATER * patched * power
    even = total_ref[pl.ds(0, FG // 2, stride=2), :]
    odd = total_ref[pl.ds(1, FG // 2, stride=2), :]
    low = iota(even.shape, 1) < FG
    out_ref[0] = jnp.where(low, even, pltpu.roll(odd, FG, 1))
    out_ref[1] = jnp.where(low, pltpu.roll(even, FG, 1), odd)


VM = pl.BlockSpec(memory_space=pltpu.VMEM)
SM = pl.BlockSpec(memory_space=pltpu.SMEM)


def sds(shape, dtype):
    return jax.ShapeDtypeStruct(shape, dtype)


def call(kernel, outs, in_specs, scratch, flops, moved):
    return pl.pallas_call(
        kernel,
        out_shape=outs,
        in_specs=in_specs,
        out_specs=jax.tree.map(lambda _: VM, outs),
        scratch_shapes=[pltpu.VMEM(s, d) for s, d in scratch],
        cost_estimate=pl.CostEstimate(flops=flops, bytes_accessed=moved, transcendentals=0),
    )


def stages():
    coefs = HB * 2 * QB
    width = FG * 2 * QB
    mega = 1 << 20
    forward = call(
        forward_kernel,
        (sds((coefs, width), BF16), sds((LOCAL * FG, width), BF16)),
        [VM] * 3,
        [((2 * HB, width), F32), ((2 * LOCAL * HB, coefs), BF16)],
        2 * 10**9, 6 * mega,
    )
    step = call(
        step_kernel,
        (sds((LOCAL * HB, coefs), BF16), sds((2 * NB, coefs // 2), BF16)),
        [SM] + [VM] * 8,
        [
            ((LOCAL * FG, width), BF16),
            ((2 * LOCAL * FG, 2 * LANES), BF16),
            ((2, FG // 2, FG * FG), F32),
        ],
        4 * 10**9, 8 * mega,
    )
    image = call(
        image_kernel, sds((LOCAL * FG, coefs), BF16), [VM] * 2, [((2 * LOCAL * HB, coefs), BF16)],
        10**8, mega,
    )
    gram = call(
        gram_kernel,
        (sds((2 * NB, coefs + 2 * NB), BF16), sds((NB, coefs), BF16)),
        [VM] * 2, [((NB, coefs), BF16)], 2 * 10**8, 2 * mega,
    )
    total = pl.pallas_call(
        sum_kernel,
        grid=(1,),
        out_shape=sds((NB, NB), F32),
        in_specs=[pl.BlockSpec((2 * NB, 2 * NB), lambda i: (0, coefs // (2 * NB)))],
        out_specs=pl.BlockSpec((NB, NB), lambda i: (0, 0)),
        name="total",
    )
    newton = call(
        newton_kernel,
        (sds((NB, coefs), BF16), sds((4 * NB, NB), BF16)),
        [VM] * 2,
        [((2 * NB, coefs), BF16)],
        10**9, mega,
    )
    density = call(
        density_kernel,
        sds((FRAGS, FG + 32, LANES), BF16),
        [SM, SM] + [VM] * 5,
        [
            ((4 * NB, coefs), BF16),
            ((2 * NB, coefs), BF16),
            ((2 * NB, width), BF16),
            ((FG, LANES), F32),
        ],
        4 * 10**9, 6 * mega,
    )
    last = call(
        last_kernel, sds((2, FG // 2, LANES), F32), [SM, SM, VM], [((FG, LANES), F32)],
        10**7, mega // 2,
    )
    return forward, step, image, gram, total, newton, density, last


def exchange(values, axis, groups=None):
    return lax.all_to_all(
        values, axis, split_axis=0, concat_axis=0, tiled=True, axis_index_groups=groups
    )


def per_device(bands_in, potential_in, hartree, patch_list):
    fwd_x, fwd_x_send, back_x, fwd_y, fwd_z, send = dft_tables()
    forward, step, image, gram, total, newton, density, last = stages()
    coefs = HB * 2 * QB
    groups = lax.axis_size("band")
    chips = groups // 2
    planes = FG // groups
    own = lax.axis_index("frag").astype(jnp.int32).reshape(1)
    near = (lax.axis_index("band") % 2).astype(jnp.int32).reshape(1)

    pot = potential_in.astype(BF16).reshape(1, planes * 4, FG * FG // 4)
    along = [[2 * z + x for z in range(chips)] for x in (0, 1)]
    pot_near = exchange(jnp.broadcast_to(pot, (chips, *pot.shape[1:])), "band", along)
    pot_near = pot_near.reshape(2 * FG, FG * FG // 4)
    pot_far = lax.ppermute(pot_near, "band", [(i, i ^ 1) for i in range(groups)])
    bands = bands_in.reshape(LOCAL * HB, coefs)
    big_y, after_y = forward(bands, fwd_x, fwd_y)
    stepped_own, stepped_send = step(
        near, after_y, pot_near, pot_far, bands, big_y, fwd_z, back_x, send
    )
    received = exchange(stepped_send.reshape(groups, 2 * LOCAL, coefs // 2), "band")
    image_send = image(stepped_own, fwd_x_send)
    parts, stepped = gram(received.reshape(2 * NB, coefs // 2), image_send)
    parts = exchange(parts.reshape(groups, planes * LOCAL, -1), "band").reshape(2 * NB, -1)
    whole = exchange(total(parts).reshape(groups, LOCAL, NB), "band").reshape(NB, NB)
    phi, inverse = newton(whole, stepped)
    phi_local = exchange(phi.reshape(groups, LOCAL, coefs), "band")
    pieces = density(patch_list, own, parts, inverse, big_y, fwd_z, hartree)
    pieces, phi_local = lax.optimization_barrier((pieces, phi_local))
    back = last(patch_list, own, exchange(pieces, "frag")).reshape(1, planes, FG * FG)
    bands_out = phi_local.transpose(1, 0, 2).astype(F32).reshape(1, LOCAL, HB * coefs)
    return (bands_out, back)


def solution(mesh):
    in_specs = (P("frag", "band", None), P("frag", "band", None), P("band", "frag", None), P())
    out_specs = (P("frag", "band", None), P("frag", "band", None))

    return jax.shard_map(
        per_device, mesh=mesh, in_specs=in_specs, out_specs=out_specs, check_vma=False
    )
```

```python
import math

import numpy as np

import jax
import jax.numpy as jnp
from jax import lax
from jax.experimental import pallas as pl
from jax.experimental.pallas import tpu as pltpu
from jax.sharding import PartitionSpec as P


FG = 64
NB = 128
NEWTON = 6
COEF = 16384
FRAGS = 16
GY = 128
GZ = 128
HB = FG // 2
QB = FG // 4

SLATER = 0.9847
SOFTEN = 0.25
STEP_TAU = 0.5
NORM_EPS = 1e-06

F32 = jnp.float32
BF16 = jnp.bfloat16
LOCAL = 4
LANES = 128


def dft_tables():
    places = np.arange(FG)
    freq_xy = np.arange(HB) - HB // 2
    freq_z = np.arange(QB) - QB // 2
    turn_xy = 2.0 * math.pi / FG * ((places[:, None] * freq_xy[None, :]) % FG)
    turn_z = 2.0 * math.pi / FG * ((freq_z[:, None] * places[None, :]) % FG)
    cos_xy, sin_xy = np.cos(turn_xy), np.sin(turn_xy)
    cos_z, sin_z = np.cos(turn_z), np.sin(turn_z)
    same = np.eye(LOCAL)
    fwd_x = np.stack([np.einsum("ab,xk->axbk", same, t) for t in (cos_xy, sin_xy)], axis=2)
    fwd_x = fwd_x.reshape(LOCAL, FG // 4, 2, 2, 2 * LOCAL * HB)
    fwd_x_send = fwd_x.transpose(1, 2, 3, 0, 4).reshape(LOCAL * FG, -1)
    fwd_x = fwd_x.transpose(2, 0, 1, 3, 4).reshape(LOCAL * FG, -1)
    back_x = np.stack([np.einsum("ab,xk->akbx", same, t) for t in (cos_xy, -sin_xy)], axis=2)
    back_x = back_x.reshape(LOCAL * HB, 2, LOCAL, FG // 4, 2, 2).transpose(0, 1, 4, 2, 3, 5)
    back_x = back_x.reshape(LOCAL * HB, 2 * LOCAL * FG)
    fwd_y = np.stack(
        [np.stack([cos_xy.T, sin_xy.T], axis=2), np.stack([-sin_xy.T, cos_xy.T], axis=2)], axis=1
    ).reshape(2 * HB, 2 * FG)
    one_z = np.block([[cos_z, sin_z], [-sin_z, cos_z]])
    fwd_z = np.einsum("ab,kz->akbz", same, one_z).reshape(LOCAL * 2 * QB, LOCAL * 2 * FG)
    send = np.einsum("gh,ab,kl->kgahbl", np.eye(2), same, np.eye(HB))
    send = send.reshape(2 * LOCAL * HB, 2 * LOCAL * HB)
    return tuple(
        jnp.asarray(t, dtype=F32).astype(BF16)
        for t in (fwd_x, fwd_x_send, back_x, fwd_y, fwd_z, send)
    )


def iota(shape, axis):
    return lax.broadcasted_iota(jnp.int32, shape, axis)


def dot(left, right):
    return jnp.dot(left, right, preferred_element_type=F32)


def dot_t(left, right):
    return lax.dot_general(left, right, (((1,), (1,)), ((), ())), preferred_element_type=F32)


def onehot(matches):
    return matches.astype(F32).astype(BF16)


def times_i(block):
    first = iota(block.shape, 1) % (2 * QB) < QB
    ahead = pltpu.roll(block, LANES - QB, 1)
    behind = pltpu.roll(block, QB, 1)
    return jnp.where(first, -ahead, behind)


def halves(values):
    upper = values.astype(BF16)
    return upper, (values - upper.astype(F32)).astype(BF16)


def forward_kernel(bands_ref, fwd_x_ref, fwd_y_ref, big_y_ref, out_ref, rows_ref, stack_ref):
    width = FG * 2 * QB
    spread = (iota((2 * FG, width), 1) // QB == iota((2 * FG, width), 0)).astype(F32).astype(BF16)
    rows_ref[...] = dot(fwd_y_ref[...], spread)
    same = iota((QB, width), 1) % QB == iota((QB, width), 0)

    @pl.loop(0, 2 * HB, unroll=8)
    def _(row):
        line = jnp.broadcast_to(rows_ref[pl.ds(row, 1), :], (QB, width))
        start = pl.multiple_of(row * QB, QB)
        big_y_ref[pl.ds(start, QB), :] = jnp.where(same, line, 0.0).astype(BF16)

    rows_n = LOCAL * HB
    stack_ref[:rows_n, :] = bands_ref[...]
    for start in range(0, HB * 2 * QB, LANES):
        block = bands_ref[:, start : start + LANES].astype(F32)
        stack_ref[rows_n:, start : start + LANES] = times_i(block).astype(BF16)
    after_x = dot(fwd_x_ref[...], stack_ref[...]).astype(BF16)

    @pl.loop(0, width // 512, unroll=4)
    def _(at):
        span = pl.ds(pl.multiple_of(at * 512, 512), 512)
        out_ref[:, span] = dot(after_x, big_y_ref[:, span]).astype(BF16)


def spread_parts(pair):
    low = iota(pair.shape, 1) < FG
    turned = pltpu.roll(pair, FG, 1)
    return jnp.where(low, pair, turned), jnp.where(low, turned, pair)


def step_kernel(
    near_at_ref, after_y_ref, near_any, far_any, bands_ref, big_y_any, fwd_z_ref, back_x_ref,
    send_ref, stepped_ref, sent_ref, back_ref, stack_ref, pots_ref, near_ref, far_ref, big_y_ref,
    sems,
):
    table_copy = pltpu.make_async_copy(big_y_any, big_y_ref, sems.at[0])
    near_copy = pltpu.make_async_copy(near_any, near_ref, sems.at[1])
    far_copy = pltpu.make_async_copy(far_any, far_ref, sems.at[2])
    near_copy.start()
    far_copy.start()
    table_copy.start()
    fwd_z = fwd_z_ref[...]
    near = near_at_ref[0]
    quarter = FG * FG // 4
    pick_shape = (FG // 2, 2 * FG)
    near_copy.wait()
    far_copy.wait()
    for at in range(4):
        pick = onehot(iota(pick_shape, 0) * 4 + at == iota(pick_shape, 1))
        span = slice(at * quarter, (at + 1) * quarter)
        pots_ref[near, :, span] = dot(pick, near_ref[...])
        pots_ref[1 - near, :, span] = dot(pick, far_ref[...])

    for at in range(FG // LOCAL):
        span = slice(at * LANES, (at + 1) * LANES)
        grid_vals = dot(after_y_ref[:, span], fwd_z) * (4.0 / FG**1.5)
        pots = []
        for half in (0, 1):
            pot = pots_ref[half, :, at * 2 * LANES : (at + 1) * 2 * LANES]
            parts = [*spread_parts(pot[:, :LANES]), *spread_parts(pot[:, LANES:])]
            pots += [jnp.concatenate(parts, axis=1)] * LOCAL
        weighted = (grid_vals * jnp.concatenate(pots, axis=0)).astype(BF16)
        back_ref[:, span] = dot_t(weighted, fwd_z).astype(BF16)

    table_copy.wait()
    rows_n = LOCAL * FG
    half_n = LOCAL * HB
    block_n = 2 * LANES
    for start in range(0, HB * 2 * QB, block_n):
        span = slice(start, start + block_n)
        block = dot_t(back_ref[...], big_y_ref[span, :])
        stack_ref[:rows_n, span] = block.astype(BF16)
        for low in range(start, start + block_n, LANES):
            turned = times_i(block[:, low - start : low - start + LANES])
            stack_ref[rows_n:, low : low + LANES] = turned.astype(BF16)
        image = dot(back_x_ref[...], stack_ref[:, span]) * (0.25 / FG**1.5)
        shape = (half_n, block_n)
        row, lane = iota(shape, 0), iota(shape, 1) + start
        mx, my = row % HB - HB // 2, lane // (2 * QB) - HB // 2
        mz = lane % QB - QB // 2
        kinetic = (mx * mx + my * my + mz * mz).astype(F32) * (16.0 / FG**2)
        bands = bands_ref[:, span].astype(F32)
        stepped_ref[:, span] = (bands - STEP_TAU * (kinetic * bands + image)).astype(BF16)

    half_w = HB * QB
    halves_of = jnp.concatenate([stepped_ref[:, :half_w], stepped_ref[:, half_w:]], axis=0)
    sent_ref[...] = dot(send_ref[...], halves_of).astype(BF16)


def image_kernel(stepped_ref, fwd_x_ref, image_ref, stack_ref):
    half_n = LOCAL * HB
    stack_ref[:half_n, :] = stepped_ref[...]
    for start in range(0, HB * 2 * QB, LANES):
        block = stepped_ref[:, start : start + LANES].astype(F32)
        stack_ref[half_n:, start : start + LANES] = times_i(block).astype(BF16)
    coefs = HB * 2 * QB
    image_ref[:, :coefs] = dot(fwd_x_ref[...], stack_ref[...]).astype(BF16)
    image_ref[:, coefs:] = jnp.zeros((2 * NB, NB), BF16)


def gram_kernel(received_any, image_any, out_any, stepped_ref, conj_ref, extra_ref, received_ref, sems):
    received_copy = pltpu.make_async_copy(received_any, received_ref, sems.at[0])
    received_copy.start()
    coefs = HB * 2 * QB
    half_w = coefs // 2
    shape = (NB, 2 * NB)
    row, col = iota(shape, 0), iota(shape, 1)
    at = row // LOCAL * 2 * LOCAL + row % LOCAL
    picks = [onehot(col == at + half * LOCAL) for half in (0, 1)]
    received_copy.wait()
    for half in (0, 1):
        rows = dot(picks[half], received_ref[...])
        stepped_ref[:, half * half_w : (half + 1) * half_w] = rows.astype(BF16)
        for start in range(0, half_w, LANES):
            block = -times_i(rows[:, start : start + LANES])
            conj_ref[:, half * half_w + start : half * half_w + start + LANES] = block.astype(BF16)
    stepped = stepped_ref[...]
    gram_re = dot_t(stepped, stepped)
    gram_im = dot_t(stepped, conj_ref[...])
    shape = (NB, NB)
    gram = jnp.where(iota(shape, 0) >= iota(shape, 1), gram_re, gram_im) * (1.0 / COEF)
    upper, lower = halves(gram)
    shape = (2 * NB, NB)
    row, col = iota(shape, 0), iota(shape, 1)
    at = col // LOCAL * 2 * LOCAL + col % LOCAL
    spread = dot(onehot(row == at), upper) + dot(onehot(row == at + LOCAL), lower)
    extra_ref[...] = spread.astype(BF16)
    extra_copy = pltpu.make_async_copy(extra_ref, out_any.at[:, coefs:], sems.at[1])
    extra_copy.start()
    extra_copy.wait()


def sum_kernel(parts_ref, out_ref):
    parts = parts_ref[...].astype(F32).reshape(HB, 2 * LOCAL, NB).sum(axis=0)
    whole = parts + pltpu.roll(parts, LOCAL, 0)
    out_ref[...] = jnp.broadcast_to(whole[None], (NB // 8, 8, NB)).reshape(NB, NB)


def complex_mul(left, right):
    turned = jnp.concatenate([-left[NB:], left[:NB]], axis=0)
    left_hi, left_lo = halves(jnp.concatenate([left, turned], axis=1))
    right_hi, right_lo = halves(right)
    first = dot(left_hi, jnp.concatenate([right_hi, right_lo], axis=1))
    return first[:, :NB] + (first[:, NB:] + dot(left_lo, right_hi))


def newton_kernel(gram_ref, stepped_ref, phi_ref, inv_ref, stack_ref):
    packed = gram_ref[...]
    flipped = packed.T
    shape = (NB, NB)
    row, col = iota(shape, 0), iota(shape, 1)
    gram_re = jnp.where(row >= col, packed, flipped)
    gram_im = jnp.where(row < col, packed, jnp.where(row > col, -flipped, 0.0))
    total = jnp.sum(gram_re * gram_re + gram_im * gram_im, axis=1, keepdims=True)
    scale = jnp.sqrt(jnp.sum(total, axis=0, keepdims=True) + NORM_EPS)
    eye = (row == col).astype(F32)
    identity = jnp.concatenate([eye, jnp.zeros(shape, F32)], axis=0)
    iter_y = jnp.concatenate([gram_re, gram_im], axis=0) / scale
    iter_z = identity
    for at in range(NEWTON):
        product = complex_mul(iter_z, iter_y) if at else iter_y
        factor = 1.5 * identity - 0.5 * product
        if at < NEWTON - 1:
            iter_y = complex_mul(iter_y, factor)
        iter_z = complex_mul(factor, iter_z) if at else factor
    inverse = iter_z / jnp.sqrt(scale)
    inv_re, inv_im = inverse[:NB].T, inverse[NB:].T
    re_hi, re_lo = halves(inv_re)
    im_hi, im_lo = halves(inv_im)
    inv_ref[...] = jnp.concatenate([re_hi, im_hi, re_lo, im_lo], axis=0)
    stack_ref[:NB, :] = stepped_ref[...]
    for start in range(0, HB * 2 * QB, LANES):
        block = stepped_ref[:, start : start + LANES].astype(F32)
        stack_ref[NB:, start : start + LANES] = times_i(block).astype(BF16)
    left = jnp.concatenate(
        [jnp.concatenate([re_hi, im_hi], axis=1), jnp.concatenate([re_lo, im_lo], axis=1)], axis=0
    )
    both = dot(left, stack_ref[...])
    phi = (both[:NB] + both[NB:]).astype(BF16)
    half_w = HB * QB
    shape = (2 * NB, NB)
    row, col = iota(shape, 0), iota(shape, 1)
    same = row // (2 * LOCAL) * LOCAL + row % LOCAL == col
    picks = [onehot(same & (row // LOCAL % 2 == half)) for half in (0, 1)]
    sent = dot(picks[0], phi[:, :half_w]) + dot(picks[1], phi[:, half_w:])
    phi_ref[...] = sent.astype(BF16)


def density_kernel(
    place_ref, own_ref, image_ref, inv_ref, big_y_ref, fwd_z_ref, tile_ref,
    out_ref, stack_ref, phi_ref, after_y_ref, dens_ref,
):
    rows_n = 2 * NB
    shape = (NB, 2 * rows_n)
    row, col = iota(shape, 0), iota(shape, 1)
    inner = col % rows_n
    picks = (inner // 8 * LOCAL + inner % LOCAL == row) & (inner // LOCAL % 2 == col // rows_n)
    spread = dot(inv_ref[...], picks.astype(F32).astype(BF16)).astype(BF16)
    stack_ref[:rows_n, :] = image_ref[:, : HB * 2 * QB]
    for start in range(0, HB * 2 * QB, LANES):
        block = image_ref[:, start : start + LANES].astype(F32)
        stack_ref[rows_n:, start : start + LANES] = times_i(block).astype(BF16)
    left = jnp.concatenate(
        [
            jnp.concatenate(
                [
                    spread[base : base + NB, at * rows_n : (at + 1) * rows_n]
                    for base in (low, low + NB)
                ],
                axis=1,
            )
            for low in (0, 2 * NB)
            for at in (0, 1)
        ],
        axis=0,
    )
    both = dot(left, stack_ref[...])
    phi_ref[...] = (both[:rows_n] + both[rows_n:]).astype(BF16)
    width = FG * 2 * QB

    @pl.loop(0, width // 512, unroll=4)
    def _(at):
        span = pl.ds(pl.multiple_of(at * 512, 512), 512)
        after_y_ref[:, span] = dot(phi_ref[...], big_y_ref[:, span]).astype(BF16)

    low = iota((1, LANES), 1) < FG

    @pl.loop(0, FG // LOCAL, unroll=4)
    def _(at):
        span = pl.ds(pl.multiple_of(at * LANES, LANES), LANES)
        grid_vals = dot(after_y_ref[:, span], fwd_z_ref[...]) * (4.0 / FG**1.5)
        square = grid_vals * grid_vals
        sums = [
            jnp.sum(square[plane * NB : (plane + 1) * NB], axis=0, keepdims=True) * (2.0 / NB)
            for plane in (0, 1)
        ]
        for y_lo in range(LOCAL):
            parts = [s[:, y_lo * LANES : (y_lo + 1) * LANES] for s in sums]
            full = [p + pltpu.roll(p, FG, 1) for p in parts]
            dens_ref[pl.ds(at * LOCAL + y_lo, 1), :] = jnp.where(low, full[0], full[1])

    own = own_ref[0]
    own_y, own_z = place_ref[own, 1], place_ref[own, 2]
    sign = place_ref[own, 0].astype(F32)
    dens = (dens_ref[...] * sign).astype(BF16)
    shape = (LANES, LANES)
    row, col = iota(shape, 0), iota(shape, 1)
    same_plane = row // FG == col // FG
    rows_shape = (FG, FG)
    rows_row, rows_col = iota(rows_shape, 0), iota(rows_shape, 1)
    for to in range(FRAGS):
        shift_y = place_ref[to, 1] - own_y + GY
        shift_z = place_ref[to, 2] - own_z + GZ
        cols = same_plane & ((col % FG + shift_z) % GZ == row % FG)
        moved = dot(dens, cols.astype(F32).astype(BF16)).astype(BF16)
        rows = (rows_row + shift_y) % GY == rows_col
        out_ref[to, :FG, :] = dot(rows.astype(F32).astype(BF16), moved).astype(BF16)
        for at, part in enumerate(halves(tile_ref[...].reshape(2 * 8, GZ))):
            out_ref[to, FG + at * 16 : FG + (at + 1) * 16, :] = part


def last_kernel(place_ref, own_ref, pieces_any, out_ref, total_ref, pieces_ref, sem):
    pieces_copy = pltpu.make_async_copy(pieces_any, pieces_ref, sem)
    pieces_copy.start()
    own = own_ref[0]
    own_y, own_z = place_ref[own, 1], place_ref[own, 2]
    pieces_copy.wait()
    patched = jnp.zeros((FG, LANES), F32)
    for at in range(FRAGS):
        patched += pieces_ref[at, :FG, :].astype(F32)
    rows = onehot((iota((FG, GY), 0) + own_y) % GY == iota((FG, GY), 1))
    shape = (GZ, LANES)
    row, col = iota(shape, 0), iota(shape, 1)
    total = jnp.zeros((FG, LANES), F32)
    tiles = pieces_ref[:, FG:, :].astype(F32)
    for plane in (0, 1):
        cols = onehot((col // FG == plane) & ((col % FG + own_z) % GZ == row))
        for part in (0, 1):
            start = part * 16 + plane * 8
            tile = tiles[:, start : start + 8, :].reshape(GY, GZ).astype(BF16)
            total += dot(dot(rows, tile).astype(BF16), cols)
    power = jnp.exp(jnp.log(patched * patched + SOFTEN) * (-1.0 / 3.0))
    total_ref[...] = total - SLATER * patched * power
    even = total_ref[pl.ds(0, FG // 2, stride=2), :]
    odd = total_ref[pl.ds(1, FG // 2, stride=2), :]
    low = iota(even.shape, 1) < FG
    planes = [jnp.where(low, even, pltpu.roll(odd, FG, 1)), jnp.where(low, pltpu.roll(even, FG, 1), odd)]
    for plane in (0, 1):
        for at in range(FG // 2):
            out_ref[plane : plane + 1, at * LANES : (at + 1) * LANES] = planes[plane][at : at + 1]


VM = pl.BlockSpec(memory_space=pltpu.VMEM)
SM = pl.BlockSpec(memory_space=pltpu.SMEM)
ANY = pl.BlockSpec(memory_space=pl.ANY)
HBM = pl.BlockSpec(memory_space=pltpu.HBM)


def sds(shape, dtype):
    return jax.ShapeDtypeStruct(shape, dtype)


def call(kernel, outs, in_specs, scratch, flops, moved, name, copies=0, out_specs=None, aliases=None):
    return pl.pallas_call(
        kernel,
        out_shape=outs,
        in_specs=in_specs,
        out_specs=out_specs or jax.tree.map(lambda _: VM, outs),
        scratch_shapes=[pltpu.VMEM(s, d) for s, d in scratch]
        + ([pltpu.SemaphoreType.DMA((copies,) if copies > 1 else ())] if copies else []),
        input_output_aliases=aliases or {},
        cost_estimate=pl.CostEstimate(flops=flops, bytes_accessed=moved, transcendentals=0),
        compiler_params=pltpu.CompilerParams(vmem_limit_bytes=GRANT.get(name, 8) << 20),
    )


GRANT = {"forward": 16, "step": 24, "density": 24}


def stages():
    coefs = HB * 2 * QB
    width = FG * 2 * QB
    mega = 1 << 20
    forward = call(
        forward_kernel,
        (sds((coefs, width), BF16), sds((LOCAL * FG, width), BF16)),
        [VM] * 3,
        [((2 * HB, width), F32), ((2 * LOCAL * HB, coefs), BF16)],
        2 * 10**9, 6 * mega, "forward",
    )
    step = call(
        step_kernel,
        (sds((LOCAL * HB, coefs), BF16), sds((2 * NB, coefs // 2), BF16)),
        [SM, VM, ANY, ANY, VM, HBM, VM, VM, VM],
        [
            ((LOCAL * FG, width), BF16),
            ((2 * LOCAL * FG, coefs), BF16),
            ((2, FG // 2, FG * FG), F32),
            ((2 * FG, FG * FG // 4), BF16),
            ((2 * FG, FG * FG // 4), BF16),
            ((coefs, width), BF16),
        ],
        4 * 10**9, 8 * mega, "step", 3,
    )
    image = call(
        image_kernel, sds((LOCAL * FG, coefs + NB), BF16), [VM] * 2,
        [((2 * LOCAL * HB, coefs), BF16)], 10**8, mega, "image",
    )
    gram = call(
        gram_kernel,
        (sds((2 * NB, coefs + NB), BF16), sds((NB, coefs), BF16)),
        [ANY, ANY],
        [((NB, coefs), BF16), ((2 * NB, NB), BF16), ((2 * NB, coefs // 2), BF16)],
        2 * 10**8, 2 * mega, "gram", 2, (ANY, VM), {1: 0},
    )
    total = pl.pallas_call(
        sum_kernel,
        grid=(1,),
        out_shape=sds((NB, NB), F32),
        in_specs=[pl.BlockSpec((2 * NB, NB), lambda i: (0, coefs // NB))],
        out_specs=pl.BlockSpec((NB, NB), lambda i: (0, 0)),
        name="total",
    )
    newton = call(
        newton_kernel,
        (sds((2 * NB, coefs // 2), BF16), sds((4 * NB, NB), BF16)),
        [VM] * 2,
        [((2 * NB, coefs), BF16)],
        10**9, mega, "newton",
    )
    density = call(
        density_kernel,
        sds((FRAGS, FG + 32, LANES), BF16),
        [SM, SM] + [VM] * 5,
        [
            ((4 * NB, coefs), BF16),
            ((2 * NB, coefs), BF16),
            ((2 * NB, width), BF16),
            ((FG, LANES), F32),
        ],
        4 * 10**9, 6 * mega, "density",
    )
    last = call(
        last_kernel, sds((2, FG * FG), F32), [SM, SM, ANY],
        [((FG, LANES), F32), ((FRAGS, FG + 32, LANES), BF16)], 10**7, mega // 2, "last", 1,
    )
    return forward, step, image, gram, total, newton, density, last


def exchange(values, axis, groups=None):
    return lax.all_to_all(
        values, axis, split_axis=0, concat_axis=0, tiled=True, axis_index_groups=groups
    )


def per_device(bands_in, potential_in, hartree, patch_list):
    fwd_x, fwd_x_send, back_x, fwd_y, fwd_z, send = dft_tables()
    forward, step, image, gram, total, newton, density, last = stages()
    coefs = HB * 2 * QB
    groups = lax.axis_size("band")
    chips = groups // 2
    planes = FG // groups
    own = lax.axis_index("frag").astype(jnp.int32).reshape(1)
    near = (lax.axis_index("band") & 1).astype(jnp.int32).reshape(1)

    pot = potential_in.astype(BF16).reshape(1, planes * 4, FG * FG // 4)
    along = [[2 * z + x for z in range(chips)] for x in (0, 1)]
    pot_near = exchange(jnp.broadcast_to(pot, (chips, *pot.shape[1:])), "band", along)
    pot_near = pot_near.reshape(2 * FG, FG * FG // 4)
    pot_far = lax.ppermute(pot_near, "band", [(i, i ^ 1) for i in range(groups)])
    bands = bands_in.reshape(LOCAL * HB, coefs)
    big_y, after_y = forward(bands, fwd_x, fwd_y)
    stepped_own, stepped_send = step(
        near, after_y, pot_near, pot_far, bands, big_y, fwd_z, back_x, send
    )
    received = exchange(stepped_send.reshape(groups, 2 * LOCAL, coefs // 2), "band")
    image_send = image(stepped_own, fwd_x_send)
    parts, stepped = gram(received.reshape(2 * NB, coefs // 2), image_send)
    parts = exchange(parts.reshape(groups, planes * LOCAL, -1), "band").reshape(2 * NB, -1)
    whole = exchange(total(parts).reshape(groups, LOCAL, NB), "band").reshape(NB, NB)
    phi, inverse = newton(whole, stepped)
    phi_local = exchange(phi.reshape(groups, 2 * LOCAL, coefs // 2), "band")
    pieces = density(patch_list, own, parts, inverse, big_y, fwd_z, hartree)
    pieces, phi_local = lax.optimization_barrier((pieces, phi_local))
    back = last(patch_list, own, exchange(pieces, "frag")).reshape(1, planes, FG * FG)
    bands_out = phi_local.reshape(groups, 2, LOCAL, coefs // 2).transpose(2, 0, 1, 3)
    bands_out = bands_out.astype(F32).reshape(1, LOCAL, HB * coefs)
    return (bands_out, back)


def solution(mesh):
    in_specs = (P("frag", "band", None), P("frag", "band", None), P("band", "frag", None), P())
    out_specs = (P("frag", "band", None), P("frag", "band", None))

    return jax.shard_map(
        per_device, mesh=mesh, in_specs=in_specs, out_specs=out_specs, check_vma=False
    )
```

```python
import math

import numpy as np

import jax
import jax.numpy as jnp
from jax import lax
from jax.experimental import pallas as pl
from jax.experimental.pallas import tpu as pltpu
from jax.sharding import PartitionSpec as P


FG = 64
NB = 128
NEWTON = 6
COEF = 16384
FRAGS = 16
GY = 128
GZ = 128
HB = FG // 2
QB = FG // 4

SLATER = 0.9847
SOFTEN = 0.25
STEP_TAU = 0.5
NORM_EPS = 1e-06

F32 = jnp.float32
BF16 = jnp.bfloat16
LOCAL = 4
LANES = 128


def dft_tables():
    places = np.arange(FG)
    freq_xy = np.arange(HB) - HB // 2
    freq_z = np.arange(QB) - QB // 2
    turn_xy = 2.0 * math.pi / FG * ((places[:, None] * freq_xy[None, :]) % FG)
    turn_z = 2.0 * math.pi / FG * ((freq_z[:, None] * places[None, :]) % FG)
    cos_xy, sin_xy = np.cos(turn_xy), np.sin(turn_xy)
    cos_z, sin_z = np.cos(turn_z), np.sin(turn_z)
    same = np.eye(LOCAL)
    fwd_x = np.stack([np.einsum("ab,xk->axbk", same, t) for t in (cos_xy, sin_xy)], axis=2)
    fwd_x = fwd_x.reshape(LOCAL, FG // 4, 2, 2, 2 * LOCAL * HB)
    fwd_x_send = fwd_x.transpose(1, 2, 3, 0, 4).reshape(LOCAL * FG, -1)
    fwd_x = fwd_x.transpose(2, 0, 1, 3, 4).reshape(LOCAL * FG, -1)
    back_x = np.stack([np.einsum("ab,xk->akbx", same, t) for t in (cos_xy, -sin_xy)], axis=2)
    back_x = back_x.reshape(LOCAL * HB, 2, LOCAL, FG // 4, 2, 2).transpose(4, 0, 1, 2, 3, 5)
    back_x = back_x.reshape(2, LOCAL * HB, LOCAL * FG)
    fwd_y = np.stack(
        [np.stack([cos_xy.T, sin_xy.T], axis=2), np.stack([-sin_xy.T, cos_xy.T], axis=2)], axis=1
    ).reshape(2 * HB, 2 * FG)
    one_z = np.block([[cos_z, sin_z], [-sin_z, cos_z]])
    fwd_z = np.einsum("ab,kz->akbz", same, one_z).reshape(LOCAL * 2 * QB, LOCAL * 2 * FG)
    send = np.einsum("gh,ab,kl->kgahbl", np.eye(2), same, np.eye(HB))
    send = send.reshape(2 * LOCAL * HB, 2 * LOCAL * HB)
    return tuple(
        jnp.asarray(t, dtype=F32).astype(BF16)
        for t in (fwd_x, fwd_x_send, back_x, fwd_y, fwd_z, send)
    )


def iota(shape, axis):
    return lax.broadcasted_iota(jnp.int32, shape, axis)


def dot(left, right):
    return jnp.dot(left, right, preferred_element_type=F32)


def dot_t(left, right):
    return lax.dot_general(left, right, (((1,), (1,)), ((), ())), preferred_element_type=F32)


def onehot(matches):
    return matches.astype(F32).astype(BF16)


def times_i(block):
    first = iota(block.shape, 1) % (2 * QB) < QB
    ahead = pltpu.roll(block, LANES - QB, 1)
    behind = pltpu.roll(block, QB, 1)
    return jnp.where(first, -ahead, behind)


def halves(values):
    upper = values.astype(BF16)
    return upper, (values - upper.astype(F32)).astype(BF16)


def forward_kernel(bands_ref, fwd_x_ref, fwd_y_ref, big_y_ref, out_ref, rows_ref, stack_ref):
    width = FG * 2 * QB
    spread = (iota((2 * FG, width), 1) // QB == iota((2 * FG, width), 0)).astype(F32).astype(BF16)
    rows_ref[...] = dot(fwd_y_ref[...], spread)
    same = iota((QB, width), 1) % QB == iota((QB, width), 0)

    @pl.loop(0, 2 * HB, unroll=8)
    def _(row):
        line = jnp.broadcast_to(rows_ref[pl.ds(row, 1), :], (QB, width))
        start = pl.multiple_of(row * QB, QB)
        big_y_ref[pl.ds(start, QB), :] = jnp.where(same, line, 0.0).astype(BF16)

    rows_n = LOCAL * HB
    stack_ref[:rows_n, :] = bands_ref[...]
    for start in range(0, HB * 2 * QB, LANES):
        block = bands_ref[:, start : start + LANES].astype(F32)
        stack_ref[rows_n:, start : start + LANES] = times_i(block).astype(BF16)
    after_x = dot(fwd_x_ref[...], stack_ref[...]).astype(BF16)
    half_n = LOCAL * FG // 2

    @pl.loop(0, width // 512, unroll=4)
    def _(at):
        span = pl.ds(pl.multiple_of(at * 512, 512), 512)
        block = dot(after_x, big_y_ref[:, span]).astype(BF16)
        out_ref[0, :, span] = block[:half_n]
        out_ref[1, :, span] = block[half_n:]


def spread_parts(pair):
    low = iota(pair.shape, 1) < FG
    turned = pltpu.roll(pair, FG, 1)
    return jnp.where(low, pair, turned), jnp.where(low, turned, pair)


def weigh_rows(at_half, after_y_ref, pot_ref, big_y_ref, fwd_z_ref, stack_ref, back_ref, pots_ref):
    fwd_z = fwd_z_ref[...]
    quarter = FG * FG // 4
    pick_shape = (FG // 2, 2 * FG)
    for at in range(4):
        pick = onehot(iota(pick_shape, 0) * 4 + at == iota(pick_shape, 1))
        pots_ref[:, at * quarter : (at + 1) * quarter] = dot(pick, pot_ref[...])

    for at in range(FG // LOCAL):
        span = slice(at * LANES, (at + 1) * LANES)
        grid_vals = dot(after_y_ref[at_half, :, span], fwd_z) * (4.0 / FG**1.5)
        pot = pots_ref[:, at * 2 * LANES : (at + 1) * 2 * LANES]
        parts = [*spread_parts(pot[:, :LANES]), *spread_parts(pot[:, LANES:])]
        pots = jnp.concatenate([jnp.concatenate(parts, axis=1)] * LOCAL, axis=0)
        back_ref[:, span] = dot_t((grid_vals * pots).astype(BF16), fwd_z).astype(BF16)

    rows_n = LOCAL * FG // 2
    block_n = 2 * LANES
    for start in range(0, HB * 2 * QB, block_n):
        span = slice(start, start + block_n)
        block = dot_t(back_ref[...], big_y_ref[span, :])
        stack_ref[:rows_n, span] = block.astype(BF16)
        for low in range(start, start + block_n, LANES):
            turned = times_i(block[:, low - start : low - start + LANES])
            stack_ref[rows_n:, low : low + LANES] = turned.astype(BF16)


def near_kernel(
    near_at_ref, after_y_ref, pot_ref, big_y_ref, fwd_z_ref, stack_ref, back_ref, pots_ref
):
    weigh_rows(
        near_at_ref[0], after_y_ref, pot_ref, big_y_ref, fwd_z_ref, stack_ref, back_ref, pots_ref
    )


def step_kernel(
    near_at_ref, after_y_ref, pot_ref, big_y_ref, fwd_z_ref, near_ref, bands_ref, back_x_ref,
    send_ref, stepped_ref, sent_ref, stack_ref, back_ref, pots_ref,
):
    near = near_at_ref[0]
    weigh_rows(
        1 - near, after_y_ref, pot_ref, big_y_ref, fwd_z_ref, stack_ref, back_ref, pots_ref
    )
    half_n = LOCAL * HB
    block_n = 2 * LANES
    for start in range(0, HB * 2 * QB, block_n):
        span = slice(start, start + block_n)
        image = dot(back_x_ref[near], near_ref[:, span])
        image = (image + dot(back_x_ref[1 - near], stack_ref[:, span])) * (0.25 / FG**1.5)
        shape = (half_n, block_n)
        row, lane = iota(shape, 0), iota(shape, 1) + start
        mx, my = row % HB - HB // 2, lane // (2 * QB) - HB // 2
        mz = lane % QB - QB // 2
        kinetic = (mx * mx + my * my + mz * mz).astype(F32) * (16.0 / FG**2)
        bands = bands_ref[:, span].astype(F32)
        stepped_ref[:, span] = (bands - STEP_TAU * (kinetic * bands + image)).astype(BF16)

    half_w = HB * QB
    halves_of = jnp.concatenate([stepped_ref[:, :half_w], stepped_ref[:, half_w:]], axis=0)
    sent_ref[...] = dot(send_ref[...], halves_of).astype(BF16)


def image_kernel(stepped_ref, fwd_x_ref, image_ref, stack_ref):
    half_n = LOCAL * HB
    stack_ref[:half_n, :] = stepped_ref[...]
    for start in range(0, HB * 2 * QB, LANES):
        block = stepped_ref[:, start : start + LANES].astype(F32)
        stack_ref[half_n:, start : start + LANES] = times_i(block).astype(BF16)
    coefs = HB * 2 * QB
    image_ref[:, :coefs] = dot(fwd_x_ref[...], stack_ref[...]).astype(BF16)
    image_ref[:, coefs:] = jnp.zeros((2 * NB, NB), BF16)


def gram_kernel(received_any, image_any, out_any, stepped_ref, conj_ref, extra_ref, received_ref, sems):
    received_copy = pltpu.make_async_copy(received_any, received_ref, sems.at[0])
    received_copy.start()
    coefs = HB * 2 * QB
    half_w = coefs // 2
    shape = (NB, 2 * NB)
    row, col = iota(shape, 0), iota(shape, 1)
    at = row // LOCAL * 2 * LOCAL + row % LOCAL
    picks = [onehot(col == at + half * LOCAL) for half in (0, 1)]
    received_copy.wait()
    for half in (0, 1):
        rows = dot(picks[half], received_ref[...])
        stepped_ref[:, half * half_w : (half + 1) * half_w] = rows.astype(BF16)
        for start in range(0, half_w, LANES):
            block = -times_i(rows[:, start : start + LANES])
            conj_ref[:, half * half_w + start : half * half_w + start + LANES] = block.astype(BF16)
    stepped = stepped_ref[...]
    gram_re = dot_t(stepped, stepped)
    gram_im = dot_t(stepped, conj_ref[...])
    shape = (NB, NB)
    gram = jnp.where(iota(shape, 0) >= iota(shape, 1), gram_re, gram_im) * (1.0 / COEF)
    upper, lower = halves(gram)
    shape = (2 * NB, NB)
    row, col = iota(shape, 0), iota(shape, 1)
    at = col // LOCAL * 2 * LOCAL + col % LOCAL
    spread = dot(onehot(row == at), upper) + dot(onehot(row == at + LOCAL), lower)
    extra_ref[...] = spread.astype(BF16)
    extra_copy = pltpu.make_async_copy(extra_ref, out_any.at[:, coefs:], sems.at[1])
    extra_copy.start()
    extra_copy.wait()


def sum_kernel(parts_ref, out_ref):
    parts = parts_ref[:, HB * 2 * QB :].astype(F32).reshape(HB, 2 * LOCAL, NB).sum(axis=0)
    whole = parts + pltpu.roll(parts, LOCAL, 0)
    out_ref[...] = jnp.broadcast_to(whole[None], (NB // 8, 8, NB)).reshape(NB, NB)


def complex_mul(left, right):
    turned = jnp.concatenate([-left[NB:], left[:NB]], axis=0)
    left_hi, left_lo = halves(jnp.concatenate([left, turned], axis=1))
    right_hi, right_lo = halves(right)
    first = dot(left_hi, jnp.concatenate([right_hi, right_lo], axis=1))
    return first[:, :NB] + (first[:, NB:] + dot(left_lo, right_hi))


def newton_kernel(gram_ref, stepped_ref, phi_ref, inv_ref, stack_ref):
    packed = gram_ref[...]
    flipped = packed.T
    shape = (NB, NB)
    row, col = iota(shape, 0), iota(shape, 1)
    gram_re = jnp.where(row >= col, packed, flipped)
    gram_im = jnp.where(row < col, packed, jnp.where(row > col, -flipped, 0.0))
    total = jnp.sum(gram_re * gram_re + gram_im * gram_im, axis=1, keepdims=True)
    scale = jnp.sqrt(jnp.sum(total, axis=0, keepdims=True) + NORM_EPS)
    eye = (row == col).astype(F32)
    identity = jnp.concatenate([eye, jnp.zeros(shape, F32)], axis=0)
    iter_y = jnp.concatenate([gram_re, gram_im], axis=0) / scale
    iter_z = identity
    for at in range(NEWTON):
        product = complex_mul(iter_z, iter_y) if at else iter_y
        factor = 1.5 * identity - 0.5 * product
        if at < NEWTON - 1:
            iter_y = complex_mul(iter_y, factor)
        iter_z = complex_mul(factor, iter_z) if at else factor
    inverse = iter_z / jnp.sqrt(scale)
    inv_re, inv_im = inverse[:NB].T, inverse[NB:].T
    re_hi, re_lo = halves(inv_re)
    im_hi, im_lo = halves(inv_im)
    inv_ref[...] = jnp.concatenate([re_hi, im_hi, re_lo, im_lo], axis=0)
    stack_ref[:NB, :] = stepped_ref[...]
    for start in range(0, HB * 2 * QB, LANES):
        block = stepped_ref[:, start : start + LANES].astype(F32)
        stack_ref[NB:, start : start + LANES] = times_i(block).astype(BF16)
    left = jnp.concatenate(
        [jnp.concatenate([re_hi, im_hi], axis=1), jnp.concatenate([re_lo, im_lo], axis=1)], axis=0
    )
    both = dot(left, stack_ref[...])
    phi = (both[:NB] + both[NB:]).astype(BF16)
    half_w = HB * QB
    shape = (2 * NB, NB)
    row, col = iota(shape, 0), iota(shape, 1)
    same = row // (2 * LOCAL) * LOCAL + row % LOCAL == col
    picks = [onehot(same & (row // LOCAL % 2 == half)) for half in (0, 1)]
    sent = dot(picks[0], phi[:, :half_w]) + dot(picks[1], phi[:, half_w:])
    phi_ref[...] = sent.astype(BF16)


def density_kernel(
    place_ref, own_ref, image_ref, inv_ref, big_y_ref, fwd_z_ref, tile_ref,
    out_ref, stack_ref, phi_ref, after_y_ref, dens_ref,
):
    rows_n = 2 * NB
    shape = (NB, 2 * rows_n)
    row, col = iota(shape, 0), iota(shape, 1)
    inner = col % rows_n
    picks = (inner // 8 * LOCAL + inner % LOCAL == row) & (inner // LOCAL % 2 == col // rows_n)
    spread = dot(inv_ref[...], picks.astype(F32).astype(BF16)).astype(BF16)
    stack_ref[:rows_n, :] = image_ref[:, : HB * 2 * QB]
    for start in range(0, HB * 2 * QB, LANES):
        block = image_ref[:, start : start + LANES].astype(F32)
        stack_ref[rows_n:, start : start + LANES] = times_i(block).astype(BF16)
    left = jnp.concatenate(
        [
            jnp.concatenate(
                [
                    spread[base : base + NB, at * rows_n : (at + 1) * rows_n]
                    for base in (low, low + NB)
                ],
                axis=1,
            )
            for low in (0, 2 * NB)
            for at in (0, 1)
        ],
        axis=0,
    )
    both = dot(left, stack_ref[...])
    phi_ref[...] = (both[:rows_n] + both[rows_n:]).astype(BF16)
    width = FG * 2 * QB

    @pl.loop(0, width // 512, unroll=4)
    def _(at):
        span = pl.ds(pl.multiple_of(at * 512, 512), 512)
        after_y_ref[:, span] = dot(phi_ref[...], big_y_ref[:, span]).astype(BF16)

    low = iota((1, LANES), 1) < FG

    @pl.loop(0, FG // LOCAL, unroll=4)
    def _(at):
        span = pl.ds(pl.multiple_of(at * LANES, LANES), LANES)
        grid_vals = dot(after_y_ref[:, span], fwd_z_ref[...]) * (4.0 / FG**1.5)
        square = grid_vals * grid_vals
        sums = [
            jnp.sum(square[plane * NB : (plane + 1) * NB], axis=0, keepdims=True) * (2.0 / NB)
            for plane in (0, 1)
        ]
        for y_lo in range(LOCAL):
            parts = [s[:, y_lo * LANES : (y_lo + 1) * LANES] for s in sums]
            full = [p + pltpu.roll(p, FG, 1) for p in parts]
            dens_ref[pl.ds(at * LOCAL + y_lo, 1), :] = jnp.where(low, full[0], full[1])

    own = own_ref[0]
    own_y, own_z = place_ref[own, 1], place_ref[own, 2]
    sign = place_ref[own, 0].astype(F32)
    dens = (dens_ref[...] * sign).astype(BF16)
    shape = (LANES, LANES)
    row, col = iota(shape, 0), iota(shape, 1)
    same_plane = row // FG == col // FG
    rows_shape = (FG, FG)
    rows_row, rows_col = iota(rows_shape, 0), iota(rows_shape, 1)
    for to in range(FRAGS):
        shift_y = place_ref[to, 1] - own_y + GY
        shift_z = place_ref[to, 2] - own_z + GZ
        cols = same_plane & ((col % FG + shift_z) % GZ == row % FG)
        moved = dot(dens, cols.astype(F32).astype(BF16)).astype(BF16)
        rows = (rows_row + shift_y) % GY == rows_col
        out_ref[to, :FG, :] = dot(rows.astype(F32).astype(BF16), moved).astype(BF16)
        for at, part in enumerate(halves(tile_ref[...].reshape(2 * 8, GZ))):
            out_ref[to, FG + at * 16 : FG + (at + 1) * 16, :] = part


def last_kernel(place_ref, own_ref, pieces_any, out_ref, total_ref, pieces_ref, sem):
    pieces_copy = pltpu.make_async_copy(pieces_any, pieces_ref, sem)
    pieces_copy.start()
    own = own_ref[0]
    own_y, own_z = place_ref[own, 1], place_ref[own, 2]
    pieces_copy.wait()
    patched = jnp.zeros((FG, LANES), F32)
    for at in range(FRAGS):
        patched += pieces_ref[at, :FG, :].astype(F32)
    rows = onehot((iota((FG, GY), 0) + own_y) % GY == iota((FG, GY), 1))
    shape = (GZ, LANES)
    row, col = iota(shape, 0), iota(shape, 1)
    total = jnp.zeros((FG, LANES), F32)
    tiles = pieces_ref[:, FG:, :].astype(F32)
    for plane in (0, 1):
        cols = onehot((col // FG == plane) & ((col % FG + own_z) % GZ == row))
        for part in (0, 1):
            start = part * 16 + plane * 8
            tile = tiles[:, start : start + 8, :].reshape(GY, GZ).astype(BF16)
            total += dot(dot(rows, tile).astype(BF16), cols)
    power = jnp.exp(jnp.log(patched * patched + SOFTEN) * (-1.0 / 3.0))
    total_ref[...] = total - SLATER * patched * power
    even = total_ref[pl.ds(0, FG // 2, stride=2), :]
    odd = total_ref[pl.ds(1, FG // 2, stride=2), :]
    low = iota(even.shape, 1) < FG
    planes = [jnp.where(low, even, pltpu.roll(odd, FG, 1)), jnp.where(low, pltpu.roll(even, FG, 1), odd)]
    for plane in (0, 1):
        for at in range(FG // 2):
            out_ref[plane : plane + 1, at * LANES : (at + 1) * LANES] = planes[plane][at : at + 1]


VM = pl.BlockSpec(memory_space=pltpu.VMEM)
SM = pl.BlockSpec(memory_space=pltpu.SMEM)
ANY = pl.BlockSpec(memory_space=pl.ANY)
HBM = pl.BlockSpec(memory_space=pltpu.HBM)


def sds(shape, dtype):
    return jax.ShapeDtypeStruct(shape, dtype)


def call(kernel, outs, in_specs, scratch, flops, moved, name, copies=0, out_specs=None, aliases=None):
    return pl.pallas_call(
        kernel,
        out_shape=outs,
        in_specs=in_specs,
        out_specs=out_specs or jax.tree.map(lambda _: VM, outs),
        scratch_shapes=[pltpu.VMEM(s, d) for s, d in scratch]
        + ([pltpu.SemaphoreType.DMA((copies,) if copies > 1 else ())] if copies else []),
        input_output_aliases=aliases or {},
        cost_estimate=pl.CostEstimate(flops=flops, bytes_accessed=moved, transcendentals=0),
        compiler_params=pltpu.CompilerParams(vmem_limit_bytes=GRANT.get(name, 8) << 20),
    )


GRANT = {"forward": 16, "near": 8, "step": 12, "density": 24}


def stages():
    coefs = HB * 2 * QB
    width = FG * 2 * QB
    mega = 1 << 20
    forward = call(
        forward_kernel,
        (sds((coefs, width), BF16), sds((2, LOCAL * FG // 2, width), BF16)),
        [VM] * 3,
        [((2 * HB, width), F32), ((2 * LOCAL * HB, coefs), BF16)],
        2 * 10**9, 6 * mega, "forward",
    )
    weigh = [
        ((LOCAL * FG // 2, width), BF16),
        ((FG // 2, FG * FG), F32),
    ]
    near = call(
        near_kernel, sds((LOCAL * FG, coefs), BF16), [SM] + [VM] * 4, weigh,
        2 * 10**9, 4 * mega, "near",
    )
    step = call(
        step_kernel,
        (sds((LOCAL * HB, coefs), BF16), sds((2 * NB, coefs // 2), BF16)),
        [SM] + [VM] * 8,
        [((LOCAL * FG, coefs), BF16)] + weigh,
        2 * 10**9, 4 * mega, "step",
    )
    image = call(
        image_kernel, sds((LOCAL * FG, coefs + NB), BF16), [VM] * 2,
        [((2 * LOCAL * HB, coefs), BF16)], 10**8, mega, "image",
    )
    gram = call(
        gram_kernel,
        (sds((2 * NB, coefs + NB), BF16), sds((NB, coefs), BF16)),
        [ANY, ANY],
        [((NB, coefs), BF16), ((2 * NB, NB), BF16), ((2 * NB, coefs // 2), BF16)],
        2 * 10**8, 2 * mega, "gram", 2, (ANY, VM), {1: 0},
    )
    total = call(
        sum_kernel, sds((NB, NB), F32), [VM], [], 10**6, mega // 8, "total",
    )
    newton = call(
        newton_kernel,
        (sds((2 * NB, coefs // 2), BF16), sds((4 * NB, NB), BF16)),
        [VM] * 2,
        [((2 * NB, coefs), BF16)],
        10**9, mega, "newton",
    )
    density = call(
        density_kernel,
        sds((FRAGS, FG + 32, LANES), BF16),
        [SM, SM] + [VM] * 5,
        [
            ((4 * NB, coefs), BF16),
            ((2 * NB, coefs), BF16),
            ((2 * NB, width), BF16),
            ((FG, LANES), F32),
        ],
        4 * 10**9, 6 * mega, "density",
    )
    last = call(
        last_kernel, sds((2, FG * FG), F32), [SM, SM, ANY],
        [((FG, LANES), F32), ((FRAGS, FG + 32, LANES), BF16)], 10**7, mega // 2, "last", 1,
    )
    return forward, near, step, image, gram, total, newton, density, last


def exchange(values, axis, groups=None):
    return lax.all_to_all(
        values, axis, split_axis=0, concat_axis=0, tiled=True, axis_index_groups=groups
    )


def per_device(bands_in, potential_in, hartree, patch_list):
    fwd_x, fwd_x_send, back_x, fwd_y, fwd_z, send = dft_tables()
    forward, near, step, image, gram, total, newton, density, last = stages()
    coefs = HB * 2 * QB
    groups = lax.axis_size("band")
    chips = groups // 2
    planes = FG // groups
    own = lax.axis_index("frag").astype(jnp.int32).reshape(1)
    near_at = (lax.axis_index("band") & 1).astype(jnp.int32).reshape(1)

    pot = potential_in.astype(BF16).reshape(1, planes * 4, FG * FG // 4)
    along = [[2 * z + x for z in range(chips)] for x in (0, 1)]
    pot_near = exchange(jnp.broadcast_to(pot, (chips, *pot.shape[1:])), "band", along)
    pot_near = pot_near.reshape(2 * FG, FG * FG // 4)
    pot_far = lax.ppermute(pot_near, "band", [(i, i ^ 1) for i in range(groups)])
    bands = bands_in.reshape(LOCAL * HB, coefs)
    big_y, after_y = forward(bands, fwd_x, fwd_y)
    near_rows = near(near_at, after_y, pot_near, big_y, fwd_z)
    stepped_own, stepped_send = step(
        near_at, after_y, pot_far, big_y, fwd_z, near_rows, bands, back_x, send
    )
    received = exchange(stepped_send.reshape(groups, 2 * LOCAL, coefs // 2), "band")
    image_send = image(stepped_own, fwd_x_send)
    parts, stepped = gram(received.reshape(2 * NB, coefs // 2), image_send)
    parts = exchange(parts.reshape(groups, planes * LOCAL, -1), "band").reshape(2 * NB, -1)
    whole = exchange(total(parts).reshape(groups, LOCAL, NB), "band").reshape(NB, NB)
    phi, inverse = newton(whole, stepped)
    phi_local = exchange(phi.reshape(groups, 2 * LOCAL, coefs // 2), "band")
    pieces = density(patch_list, own, parts, inverse, big_y, fwd_z, hartree)
    pieces, phi_local = lax.optimization_barrier((pieces, phi_local))
    back = last(patch_list, own, exchange(pieces, "frag")).reshape(1, planes, FG * FG)
    bands_out = phi_local.reshape(groups, 2, LOCAL, coefs // 2).transpose(2, 0, 1, 3)
    bands_out = bands_out.astype(F32).reshape(1, LOCAL, HB * coefs)
    return (bands_out, back)


def solution(mesh):
    in_specs = (P("frag", "band", None), P("frag", "band", None), P("band", "frag", None), P())
    out_specs = (P("frag", "band", None), P("frag", "band", None))

    return jax.shard_map(
        per_device, mesh=mesh, in_specs=in_specs, out_specs=out_specs, check_vma=False
    )
```

```python
import math

import numpy as np

import jax
import jax.numpy as jnp
from jax import lax
from jax.experimental import pallas as pl
from jax.experimental.pallas import tpu as pltpu
from jax.sharding import PartitionSpec as P


FG = 64
NB = 128
NEWTON = 6
COEF = 16384
FRAGS = 16
GY = 128
GZ = 128
HB = FG // 2
QB = FG // 4

SLATER = 0.9847
SOFTEN = 0.25
STEP_TAU = 0.5
NORM_EPS = 1e-06

F32 = jnp.float32
BF16 = jnp.bfloat16
LOCAL = 4
LANES = 128


def dft_tables():
    places = np.arange(FG)
    freq_xy = np.arange(HB) - HB // 2
    freq_z = np.arange(QB) - QB // 2
    turn_xy = 2.0 * math.pi / FG * ((places[:, None] * freq_xy[None, :]) % FG)
    turn_z = 2.0 * math.pi / FG * ((freq_z[:, None] * places[None, :]) % FG)
    cos_xy, sin_xy = np.cos(turn_xy), np.sin(turn_xy)
    cos_z, sin_z = np.cos(turn_z), np.sin(turn_z)
    same = np.eye(LOCAL)
    fwd_x = np.stack([np.einsum("ab,xk->axbk", same, t) for t in (cos_xy, sin_xy)], axis=2)
    fwd_x = fwd_x.reshape(LOCAL * FG, 2 * LOCAL * HB)
    fwd_x_send = fwd_x.reshape(LOCAL, FG // 2, 2, -1).transpose(1, 2, 0, 3)
    fwd_x_send = fwd_x_send.reshape(LOCAL * FG, -1)
    back_x = np.stack([np.einsum("ab,xk->akbx", same, t) for t in (cos_xy, -sin_xy)], axis=2)
    back_x = back_x.reshape(LOCAL * HB, 2 * LOCAL * FG)
    fwd_y = np.stack(
        [np.stack([cos_xy.T, sin_xy.T], axis=2), np.stack([-sin_xy.T, cos_xy.T], axis=2)], axis=1
    ).reshape(2 * HB, 2 * FG)
    one_z = np.block([[cos_z, sin_z], [-sin_z, cos_z]])
    fwd_z = np.einsum("ab,kz->akbz", same, one_z).reshape(LOCAL * 2 * QB, LOCAL * 2 * FG)
    send = np.einsum("gh,ab,kl->kgahbl", np.eye(2), same, np.eye(HB))
    send = send.reshape(2 * LOCAL * HB, 2 * LOCAL * HB)
    return tuple(
        jnp.asarray(t, dtype=F32).astype(BF16)
        for t in (fwd_x, fwd_x_send, back_x, fwd_y, fwd_z, send)
    )


def iota(shape, axis):
    return lax.broadcasted_iota(jnp.int32, shape, axis)


def dot(left, right):
    return jnp.dot(left, right, preferred_element_type=F32)


def dot_t(left, right):
    return lax.dot_general(left, right, (((1,), (1,)), ((), ())), preferred_element_type=F32)


def onehot(matches):
    return matches.astype(F32).astype(BF16)


def times_i(block):
    first = iota(block.shape, 1) % (2 * QB) < QB
    ahead = pltpu.roll(block, LANES - QB, 1)
    behind = pltpu.roll(block, QB, 1)
    return jnp.where(first, -ahead, behind)


def halves(values):
    upper = values.astype(BF16)
    return upper, (values - upper.astype(F32)).astype(BF16)


def forward_kernel(bands_ref, fwd_x_ref, fwd_y_ref, big_y_ref, out_ref, rows_ref, stack_ref):
    width = FG * 2 * QB
    half_w = width // 2
    spread = onehot(iota((2 * FG, width), 1) // QB == iota((2 * FG, width), 0))
    rows_ref[...] = dot(fwd_y_ref[...], spread)
    same = iota((QB, width), 1) % QB == iota((QB, width), 0)

    @pl.loop(0, 2 * HB, unroll=8)
    def _(row):
        line = jnp.broadcast_to(rows_ref[pl.ds(row, 1), :], (QB, width))
        start = pl.multiple_of(row * QB, QB)
        lines = jnp.where(same, line, 0.0).astype(BF16)
        for at in range(8):
            block = lines[:, at * 256 : (at + 1) * 256]
            big_y_ref[at % 2, pl.ds(start, QB), at // 2 * 256 : (at // 2 + 1) * 256] = block

    rows_n = LOCAL * HB
    stack_ref[:rows_n, :] = bands_ref[...]
    for start in range(0, HB * 2 * QB, LANES):
        block = bands_ref[:, start : start + LANES].astype(F32)
        stack_ref[rows_n:, start : start + LANES] = times_i(block).astype(BF16)
    after_x = dot(fwd_x_ref[...], stack_ref[...]).astype(BF16)
    for half in (0, 1):
        for start in range(0, half_w, 512):
            span = slice(start, start + 512)
            out_ref[half, :, span] = dot(after_x, big_y_ref[half, :, span]).astype(BF16)


def spread_parts(pair):
    low = iota(pair.shape, 1) < FG
    turned = pltpu.roll(pair, FG, 1)
    return jnp.where(low, pair, turned), jnp.where(low, turned, pair)


def weigh_half(half, after_y_ref, pot_ref, fwd_z_ref, back_ref, pots_ref):
    fwd_z = fwd_z_ref[...]
    quarter = FG * FG // 8
    pick_shape = (FG, LOCAL * FG)
    for at in range(4):
        pick = onehot(iota(pick_shape, 0) * 4 + at == iota(pick_shape, 1))
        pots_ref[:, at * quarter : (at + 1) * quarter] = dot(pick, pot_ref[...])

    for at in range(FG // LOCAL // 2):
        span = slice(at * LANES, (at + 1) * LANES)
        grid_vals = dot(after_y_ref[half, :, span], fwd_z) * (4.0 / FG**1.5)
        pot = pots_ref[:, at * 2 * LANES : (at + 1) * 2 * LANES]
        parts = [*spread_parts(pot[:, :LANES]), *spread_parts(pot[:, LANES:])]
        pots = jnp.concatenate([jnp.concatenate(parts, axis=1)] * LOCAL, axis=0)
        back_ref[:, span] = dot_t((grid_vals * pots).astype(BF16), fwd_z).astype(BF16)


def near_kernel(
    near_at_ref, after_y_ref, pot_ref, big_y_ref, fwd_z_ref, sum_ref, back_ref, pots_ref
):
    near = near_at_ref[0]
    weigh_half(near, after_y_ref, pot_ref, fwd_z_ref, back_ref, pots_ref)
    block_n = 2 * LANES
    for start in range(0, HB * 2 * QB, block_n):
        span = slice(start, start + block_n)
        sum_ref[:, span] = dot_t(back_ref[...], big_y_ref[near, span, :])


def step_kernel(
    near_at_ref, after_y_ref, pot_ref, big_y_ref, fwd_z_ref, sum_ref, bands_ref, back_x_ref,
    send_ref, stepped_ref, sent_ref, stack_ref, back_ref, pots_ref,
):
    far = 1 - near_at_ref[0]
    weigh_half(far, after_y_ref, pot_ref, fwd_z_ref, back_ref, pots_ref)
    rows_n = LOCAL * FG
    half_n = LOCAL * HB
    block_n = 2 * LANES
    for start in range(0, HB * 2 * QB, block_n):
        span = slice(start, start + block_n)
        block = sum_ref[:, span] + dot_t(back_ref[...], big_y_ref[far, span, :])
        stack_ref[:rows_n, span] = block.astype(BF16)
        for low in range(start, start + block_n, LANES):
            turned = times_i(block[:, low - start : low - start + LANES])
            stack_ref[rows_n:, low : low + LANES] = turned.astype(BF16)
        image = dot(back_x_ref[...], stack_ref[:, span]) * (0.25 / FG**1.5)
        shape = (half_n, block_n)
        row, lane = iota(shape, 0), iota(shape, 1) + start
        mx, my = row % HB - HB // 2, lane // (2 * QB) - HB // 2
        mz = lane % QB - QB // 2
        kinetic = (mx * mx + my * my + mz * mz).astype(F32) * (16.0 / FG**2)
        bands = bands_ref[:, span].astype(F32)
        stepped_ref[:, span] = (bands - STEP_TAU * (kinetic * bands + image)).astype(BF16)

    half_w = HB * QB
    halves_of = jnp.concatenate([stepped_ref[:, :half_w], stepped_ref[:, half_w:]], axis=0)
    sent_ref[...] = dot(send_ref[...], halves_of).astype(BF16)


def image_kernel(stepped_ref, fwd_x_ref, image_ref, stack_ref):
    half_n = LOCAL * HB
    stack_ref[:half_n, :] = stepped_ref[...]
    for start in range(0, HB * 2 * QB, LANES):
        block = stepped_ref[:, start : start + LANES].astype(F32)
        stack_ref[half_n:, start : start + LANES] = times_i(block).astype(BF16)
    coefs = HB * 2 * QB
    image_ref[:, :coefs] = dot(fwd_x_ref[...], stack_ref[...]).astype(BF16)
    image_ref[:, coefs:] = jnp.zeros((2 * NB, NB), BF16)


def gram_kernel(received_any, image_any, out_any, stepped_ref, conj_ref, extra_ref, received_ref, sems):
    received_copy = pltpu.make_async_copy(received_any, received_ref, sems.at[0])
    received_copy.start()
    coefs = HB * 2 * QB
    half_w = coefs // 2
    shape = (NB, 2 * NB)
    row, col = iota(shape, 0), iota(shape, 1)
    at = row // LOCAL * 2 * LOCAL + row % LOCAL
    picks = [onehot(col == at + half * LOCAL) for half in (0, 1)]
    received_copy.wait()
    for half in (0, 1):
        rows = dot(picks[half], received_ref[...])
        stepped_ref[:, half * half_w : (half + 1) * half_w] = rows.astype(BF16)
        for start in range(0, half_w, LANES):
            block = -times_i(rows[:, start : start + LANES])
            conj_ref[:, half * half_w + start : half * half_w + start + LANES] = block.astype(BF16)
    stepped = stepped_ref[...]
    gram_re = dot_t(stepped, stepped)
    gram_im = dot_t(stepped, conj_ref[...])
    shape = (NB, NB)
    gram = jnp.where(iota(shape, 0) >= iota(shape, 1), gram_re, gram_im) * (1.0 / COEF)
    upper, lower = halves(gram)
    shape = (2 * NB, NB)
    row, col = iota(shape, 0), iota(shape, 1)
    at = col // LOCAL * 2 * LOCAL + col % LOCAL
    spread = dot(onehot(row == at), upper) + dot(onehot(row == at + LOCAL), lower)
    extra_ref[...] = spread.astype(BF16)
    extra_copy = pltpu.make_async_copy(extra_ref, out_any.at[:, coefs:], sems.at[1])
    extra_copy.start()
    extra_copy.wait()


def sum_kernel(parts_ref, out_ref):
    parts = parts_ref[:, HB * 2 * QB :].astype(F32).reshape(HB, 2 * LOCAL, NB).sum(axis=0)
    whole = parts + pltpu.roll(parts, LOCAL, 0)
    out_ref[...] = jnp.broadcast_to(whole[None], (NB // 8, 8, NB)).reshape(NB, NB)


def complex_mul(left, right):
    turned = jnp.concatenate([-left[NB:], left[:NB]], axis=0)
    left_hi, left_lo = halves(jnp.concatenate([left, turned], axis=1))
    right_hi, right_lo = halves(right)
    first = dot(left_hi, jnp.concatenate([right_hi, right_lo], axis=1))
    return first[:, :NB] + (first[:, NB:] + dot(left_lo, right_hi))


def newton_kernel(gram_ref, stepped_ref, phi_ref, inv_ref, stack_ref):
    packed = gram_ref[...]
    flipped = packed.T
    shape = (NB, NB)
    row, col = iota(shape, 0), iota(shape, 1)
    gram_re = jnp.where(row >= col, packed, flipped)
    gram_im = jnp.where(row < col, packed, jnp.where(row > col, -flipped, 0.0))
    total = jnp.sum(gram_re * gram_re + gram_im * gram_im, axis=1, keepdims=True)
    scale = jnp.sqrt(jnp.sum(total, axis=0, keepdims=True) + NORM_EPS)
    eye = (row == col).astype(F32)
    identity = jnp.concatenate([eye, jnp.zeros(shape, F32)], axis=0)
    iter_y = jnp.concatenate([gram_re, gram_im], axis=0) / scale
    iter_z = identity
    for at in range(NEWTON):
        product = complex_mul(iter_z, iter_y) if at else iter_y
        factor = 1.5 * identity - 0.5 * product
        if at < NEWTON - 1:
            iter_y = complex_mul(iter_y, factor)
        iter_z = complex_mul(factor, iter_z) if at else factor
    inverse = iter_z / jnp.sqrt(scale)
    inv_re, inv_im = inverse[:NB].T, inverse[NB:].T
    re_hi, re_lo = halves(inv_re)
    im_hi, im_lo = halves(inv_im)
    inv_ref[...] = jnp.concatenate([re_hi, im_hi, re_lo, im_lo], axis=0)
    stack_ref[:NB, :] = stepped_ref[...]
    for start in range(0, HB * 2 * QB, LANES):
        block = stepped_ref[:, start : start + LANES].astype(F32)
        stack_ref[NB:, start : start + LANES] = times_i(block).astype(BF16)
    left = jnp.concatenate(
        [jnp.concatenate([re_hi, im_hi], axis=1), jnp.concatenate([re_lo, im_lo], axis=1)], axis=0
    )
    both = dot(left, stack_ref[...])
    phi = (both[:NB] + both[NB:]).astype(BF16)
    half_w = HB * QB
    shape = (2 * NB, NB)
    row, col = iota(shape, 0), iota(shape, 1)
    same = row // (2 * LOCAL) * LOCAL + row % LOCAL == col
    picks = [onehot(same & (row // LOCAL % 2 == half)) for half in (0, 1)]
    sent = dot(picks[0], phi[:, :half_w]) + dot(picks[1], phi[:, half_w:])
    phi_ref[...] = sent.astype(BF16)


def density_kernel(
    place_ref, own_ref, image_ref, inv_ref, big_y_ref, fwd_z_ref, tile_ref,
    out_ref, stack_ref, phi_ref, after_y_ref, dens_ref,
):
    rows_n = 2 * NB
    shape = (NB, 2 * rows_n)
    row, col = iota(shape, 0), iota(shape, 1)
    inner = col % rows_n
    picks = (inner // 8 * LOCAL + inner % LOCAL == row) & (inner // LOCAL % 2 == col // rows_n)
    spread = dot(inv_ref[...], picks.astype(F32).astype(BF16)).astype(BF16)
    stack_ref[:rows_n, :] = image_ref[:, : HB * 2 * QB]
    for start in range(0, HB * 2 * QB, LANES):
        block = image_ref[:, start : start + LANES].astype(F32)
        stack_ref[rows_n:, start : start + LANES] = times_i(block).astype(BF16)
    left = jnp.concatenate(
        [
            jnp.concatenate(
                [
                    spread[base : base + NB, at * rows_n : (at + 1) * rows_n]
                    for base in (low, low + NB)
                ],
                axis=1,
            )
            for low in (0, 2 * NB)
            for at in (0, 1)
        ],
        axis=0,
    )
    both = dot(left, stack_ref[...])
    phi_ref[...] = (both[:rows_n] + both[rows_n:]).astype(BF16)
    half_w = FG * QB
    for half in (0, 1):
        for start in range(0, half_w, 512):
            block = dot(phi_ref[...], big_y_ref[half, :, start : start + 512])
            for low in (0, 256):
                at = (start + low) * 2 + half * 256
                after_y_ref[:, at : at + 256] = block[:, low : low + 256].astype(BF16)

    low = iota((1, LANES), 1) < FG

    @pl.loop(0, FG // LOCAL, unroll=4)
    def _(at):
        span = pl.ds(pl.multiple_of(at * LANES, LANES), LANES)
        grid_vals = dot(after_y_ref[:, span], fwd_z_ref[...]) * (4.0 / FG**1.5)
        square = grid_vals * grid_vals
        sums = [
            jnp.sum(square[plane * NB : (plane + 1) * NB], axis=0, keepdims=True) * (2.0 / NB)
            for plane in (0, 1)
        ]
        for y_lo in range(LOCAL):
            parts = [s[:, y_lo * LANES : (y_lo + 1) * LANES] for s in sums]
            full = [p + pltpu.roll(p, FG, 1) for p in parts]
            dens_ref[pl.ds(at * LOCAL + y_lo, 1), :] = jnp.where(low, full[0], full[1])

    own = own_ref[0]
    own_y, own_z = place_ref[own, 1], place_ref[own, 2]
    sign = place_ref[own, 0].astype(F32)
    dens = (dens_ref[...] * sign).astype(BF16)
    shape = (LANES, LANES)
    row, col = iota(shape, 0), iota(shape, 1)
    same_plane = row // FG == col // FG
    rows_shape = (FG, FG)
    rows_row, rows_col = iota(rows_shape, 0), iota(rows_shape, 1)
    tiles = [jnp.concatenate(halves(tile_ref[plane]), axis=0) for plane in (0, 1)]
    for to in range(FRAGS):
        shift_y = place_ref[to, 1] - own_y + GY
        shift_z = place_ref[to, 2] - own_z + GZ
        cols = same_plane & ((col % FG + shift_z) % GZ == row % FG)
        moved = dot(dens, cols.astype(F32).astype(BF16)).astype(BF16)
        rows = (rows_row + shift_y) % GY == rows_col
        out_ref[to, :FG, :] = dot(rows.astype(F32).astype(BF16), moved).astype(BF16)
        to_z = place_ref[to, 2]
        tile = jnp.zeros((2 * 8, LANES), F32)
        for plane in (0, 1):
            cols = onehot((col // FG == plane) & ((col % FG + to_z) % GZ == row))
            tile += dot(tiles[plane], cols)
        out_ref[to, FG:, :] = tile.astype(BF16)


def last_kernel(place_ref, own_ref, pieces_any, out_ref, total_ref, pieces_ref, sem):
    pieces_copy = pltpu.make_async_copy(pieces_any, pieces_ref, sem)
    pieces_copy.start()
    own = own_ref[0]
    own_y = place_ref[own, 1]
    pieces_copy.wait()
    patched = jnp.zeros((FG, LANES), F32)
    for at in range(FRAGS):
        patched += pieces_ref[at, :FG, :].astype(F32)
    rows = onehot((iota((FG, GY), 0) + own_y) % GY == iota((FG, GY), 1))
    tiles = pieces_ref[:, FG:, :].astype(F32)
    total = jnp.zeros((FG, LANES), F32)
    for part in (0, 1):
        tile = tiles[:, part * 8 : (part + 1) * 8, :].reshape(GY, LANES)
        total += dot(rows, tile.astype(BF16))
    power = jnp.exp(jnp.log(patched * patched + SOFTEN) * (-1.0 / 3.0))
    total_ref[...] = total - SLATER * patched * power
    even = total_ref[pl.ds(0, FG // 2, stride=2), :]
    odd = total_ref[pl.ds(1, FG // 2, stride=2), :]
    low = iota(even.shape, 1) < FG
    planes = [jnp.where(low, even, pltpu.roll(odd, FG, 1)), jnp.where(low, pltpu.roll(even, FG, 1), odd)]
    for plane in (0, 1):
        for at in range(FG // 2):
            out_ref[plane : plane + 1, at * LANES : (at + 1) * LANES] = planes[plane][at : at + 1]


VM = pl.BlockSpec(memory_space=pltpu.VMEM)
SM = pl.BlockSpec(memory_space=pltpu.SMEM)
ANY = pl.BlockSpec(memory_space=pl.ANY)
HBM = pl.BlockSpec(memory_space=pltpu.HBM)


def sds(shape, dtype):
    return jax.ShapeDtypeStruct(shape, dtype)


def call(kernel, outs, in_specs, scratch, flops, moved, name, copies=0, out_specs=None, aliases=None):
    return pl.pallas_call(
        kernel,
        out_shape=outs,
        in_specs=in_specs,
        out_specs=out_specs or jax.tree.map(lambda _: VM, outs),
        scratch_shapes=[pltpu.VMEM(s, d) for s, d in scratch]
        + ([pltpu.SemaphoreType.DMA((copies,) if copies > 1 else ())] if copies else []),
        input_output_aliases=aliases or {},
        cost_estimate=pl.CostEstimate(flops=flops, bytes_accessed=moved, transcendentals=0),
        compiler_params=pltpu.CompilerParams(vmem_limit_bytes=GRANT.get(name, 8) << 20),
    )


GRANT = {"forward": 16, "near": 8, "step": 10, "density": 24}


def stages():
    coefs = HB * 2 * QB
    width = FG * 2 * QB
    mega = 1 << 20
    forward = call(
        forward_kernel,
        (sds((2, coefs, width // 2), BF16), sds((2, LOCAL * FG, width // 2), BF16)),
        [VM] * 3,
        [((2 * HB, width), F32), ((2 * LOCAL * HB, coefs), BF16)],
        2 * 10**9, 6 * mega, "forward",
    )
    weigh = [
        ((LOCAL * FG, width // 2), BF16),
        ((FG, FG * FG // 2), F32),
    ]
    near = call(
        near_kernel, sds((LOCAL * FG, coefs), F32), [SM] + [VM] * 4, weigh,
        2 * 10**9, 4 * mega, "near",
    )
    step = call(
        step_kernel,
        (sds((LOCAL * HB, coefs), BF16), sds((2 * NB, coefs // 2), BF16)),
        [SM] + [VM] * 8,
        [((2 * LOCAL * FG, coefs), BF16)] + weigh,
        2 * 10**9, 4 * mega, "step",
    )
    image = call(
        image_kernel, sds((LOCAL * FG, coefs + NB), BF16), [VM] * 2,
        [((2 * LOCAL * HB, coefs), BF16)], 10**8, mega, "image",
    )
    gram = call(
        gram_kernel,
        (sds((2 * NB, coefs + NB), BF16), sds((NB, coefs), BF16)),
        [ANY, ANY],
        [((NB, coefs), BF16), ((2 * NB, NB), BF16), ((2 * NB, coefs // 2), BF16)],
        2 * 10**8, 2 * mega, "gram", 2, (ANY, VM), {1: 0},
    )
    total = call(
        sum_kernel, sds((NB, NB), F32), [VM], [], 10**6, mega // 8, "total",
    )
    newton = call(
        newton_kernel,
        (sds((2 * NB, coefs // 2), BF16), sds((4 * NB, NB), BF16)),
        [VM] * 2,
        [((2 * NB, coefs), BF16)],
        10**9, mega, "newton",
    )
    density = call(
        density_kernel,
        sds((FRAGS, FG + 16, LANES), BF16),
        [SM, SM] + [VM] * 5,
        [
            ((4 * NB, coefs), BF16),
            ((2 * NB, coefs), BF16),
            ((2 * NB, width), BF16),
            ((FG, LANES), F32),
        ],
        4 * 10**9, 6 * mega, "density",
    )
    last = call(
        last_kernel, sds((2, FG * FG), F32), [SM, SM, ANY],
        [((FG, LANES), F32), ((FRAGS, FG + 16, LANES), BF16)], 10**7, mega // 2, "last", 1,
    )
    return forward, near, step, image, gram, total, newton, density, last


def exchange(values, axis):
    return lax.all_to_all(values, axis, split_axis=0, concat_axis=0, tiled=True)


def per_device(bands_in, potential_in, hartree, patch_list):
    fwd_x, fwd_x_send, back_x, fwd_y, fwd_z, send = dft_tables()
    forward, near, step, image, gram, total, newton, density, last = stages()
    coefs = HB * 2 * QB
    groups = lax.axis_size("band")
    chips = groups // 2
    planes = FG // groups
    own = lax.axis_index("frag").astype(jnp.int32).reshape(1)
    near_at = (lax.axis_index("band") & 1).astype(jnp.int32).reshape(1)

    pot = potential_in.astype(BF16).reshape(planes * 4, FG * FG // 4)
    pot = jnp.stack([pot[:, : FG * FG // 8], pot[:, FG * FG // 8 :]])[None]
    pot = jnp.broadcast_to(pot, (chips, *pot.shape[1:])).reshape(groups, *pot.shape[2:])
    pot_near = exchange(pot, "band").reshape(4 * FG, FG * FG // 8)
    pot_far = lax.ppermute(pot_near, "band", [(i, i ^ 1) for i in range(groups)])
    bands = bands_in.reshape(LOCAL * HB, coefs)
    big_y, after_y = forward(bands, fwd_x, fwd_y)
    near_rows = near(near_at, after_y, pot_near, big_y, fwd_z)
    stepped_own, stepped_send = step(
        near_at, after_y, pot_far, big_y, fwd_z, near_rows, bands, back_x, send
    )
    received = exchange(stepped_send.reshape(groups, 2 * LOCAL, coefs // 2), "band")
    image_send = image(stepped_own, fwd_x_send)
    parts, stepped = gram(received.reshape(2 * NB, coefs // 2), image_send)
    parts = exchange(parts.reshape(groups, planes * LOCAL, -1), "band").reshape(2 * NB, -1)
    whole = exchange(total(parts).reshape(groups, LOCAL, NB), "band").reshape(NB, NB)
    phi, inverse = newton(whole, stepped)
    phi_local = exchange(phi.reshape(groups, 2 * LOCAL, coefs // 2), "band")
    pieces = density(patch_list, own, parts, inverse, big_y, fwd_z, hartree)
    pieces, phi_local = lax.optimization_barrier((pieces, phi_local))
    back = last(patch_list, own, exchange(pieces, "frag")).reshape(1, planes, FG * FG)
    bands_out = phi_local.reshape(groups, 2, LOCAL, coefs // 2).transpose(2, 0, 1, 3)
    bands_out = bands_out.astype(F32).reshape(1, LOCAL, HB * coefs)
    return (bands_out, back)


def solution(mesh):
    in_specs = (P("frag", "band", None), P("frag", "band", None), P("band", "frag", None), P())
    out_specs = (P("frag", "band", None), P("frag", "band", None))

    return jax.shard_map(
        per_device, mesh=mesh, in_specs=in_specs, out_specs=out_specs, check_vma=False
    )
```

```python
import math

import numpy as np

import jax
import jax.numpy as jnp
from jax import lax
from jax.experimental import pallas as pl
from jax.experimental.pallas import tpu as pltpu
from jax.sharding import PartitionSpec as P


FG = 64
NB = 128
NEWTON = 6
COEF = 16384
FRAGS = 16
GY = 128
GZ = 128
HB = FG // 2
QB = FG // 4

SLATER = 0.9847
SOFTEN = 0.25
STEP_TAU = 0.5
NORM_EPS = 1e-06

F32 = jnp.float32
BF16 = jnp.bfloat16
LOCAL = 4
LANES = 128


def dft_tables():
    places = np.arange(FG)
    freq_xy = np.arange(HB) - HB // 2
    freq_z = np.arange(QB) - QB // 2
    turn_xy = 2.0 * math.pi / FG * ((places[:, None] * freq_xy[None, :]) % FG)
    turn_z = 2.0 * math.pi / FG * ((freq_z[:, None] * places[None, :]) % FG)
    cos_xy, sin_xy = np.cos(turn_xy), np.sin(turn_xy)
    cos_z, sin_z = np.cos(turn_z), np.sin(turn_z)
    same = np.eye(LOCAL)
    fwd_x = np.stack([np.einsum("ab,xk->axbk", same, t) for t in (cos_xy, sin_xy)], axis=2)
    fwd_x = fwd_x.reshape(LOCAL * FG, 2 * LOCAL * HB)
    fwd_x_send = fwd_x.reshape(LOCAL, FG // 2, 2, -1).transpose(1, 2, 0, 3)
    fwd_x_send = fwd_x_send.reshape(LOCAL * FG, -1)
    back_x = np.stack([np.einsum("ab,xk->akbx", same, t) for t in (cos_xy, -sin_xy)], axis=2)
    back_x = back_x.reshape(LOCAL * HB, 2 * LOCAL * FG)
    fwd_y = np.stack(
        [np.stack([cos_xy.T, sin_xy.T], axis=2), np.stack([-sin_xy.T, cos_xy.T], axis=2)], axis=1
    ).reshape(2 * HB, 2 * FG)
    one_z = np.block([[cos_z, sin_z], [-sin_z, cos_z]])
    fwd_z = np.einsum("ab,kz->akbz", same, one_z).reshape(LOCAL * 2 * QB, LOCAL * 2 * FG)
    send = np.einsum("gh,ab,kl->kgahbl", np.eye(2), same, np.eye(HB))
    send = send.reshape(2 * LOCAL * HB, 2 * LOCAL * HB)
    return tuple(
        jnp.asarray(t, dtype=F32).astype(BF16)
        for t in (fwd_x, fwd_x_send, back_x, fwd_y, fwd_z, send)
    )


def iota(shape, axis):
    return lax.broadcasted_iota(jnp.int32, shape, axis)


def dot(left, right):
    return jnp.dot(left, right, preferred_element_type=F32)


def dot_t(left, right):
    return lax.dot_general(left, right, (((1,), (1,)), ((), ())), preferred_element_type=F32)


def onehot(matches):
    return matches.astype(F32).astype(BF16)


def times_i(block):
    first = iota(block.shape, 1) % (2 * QB) < QB
    ahead = pltpu.roll(block, LANES - QB, 1)
    behind = pltpu.roll(block, QB, 1)
    return jnp.where(first, -ahead, behind)


def halves(values):
    upper = values.astype(BF16)
    return upper, (values - upper.astype(F32)).astype(BF16)


def forward_kernel(bands_ref, fwd_x_ref, fwd_y_ref, big_y_ref, out_ref, rows_ref, stack_ref):
    width = FG * 2 * QB
    half_w = width // 2
    spread = onehot(iota((2 * FG, width), 1) // QB == iota((2 * FG, width), 0))
    rows_ref[...] = dot(fwd_y_ref[...], spread)
    same = iota((QB, width), 1) % QB == iota((QB, width), 0)

    @pl.loop(0, 2 * HB, unroll=8)
    def _(row):
        line = jnp.broadcast_to(rows_ref[pl.ds(row, 1), :], (QB, width))
        start = pl.multiple_of(row * QB, QB)
        lines = jnp.where(same, line, 0.0).astype(BF16)
        for at in range(8):
            block = lines[:, at * 256 : (at + 1) * 256]
            big_y_ref[at % 2, pl.ds(start, QB), at // 2 * 256 : (at // 2 + 1) * 256] = block

    rows_n = LOCAL * HB
    stack_ref[:rows_n, :] = bands_ref[...]
    for start in range(0, HB * 2 * QB, LANES):
        block = bands_ref[:, start : start + LANES].astype(F32)
        stack_ref[rows_n:, start : start + LANES] = times_i(block).astype(BF16)
    after_x = dot(fwd_x_ref[...], stack_ref[...]).astype(BF16)
    for half in (0, 1):
        for start in range(0, half_w, 512):
            span = slice(start, start + 512)
            out_ref[half, :, span] = dot(after_x, big_y_ref[half, :, span]).astype(BF16)


def spread_parts(pair):
    low = iota(pair.shape, 1) < FG
    turned = pltpu.roll(pair, FG, 1)
    return jnp.where(low, pair, turned), jnp.where(low, turned, pair)


def weigh_half(half, after_y_ref, pot_ref, fwd_z_ref, back_ref, pots_ref):
    fwd_z = fwd_z_ref[...]
    quarter = FG * FG // 8
    pick_shape = (FG, LOCAL * FG)
    for at in range(4):
        pick = onehot(iota(pick_shape, 0) * 4 + at == iota(pick_shape, 1))
        pots_ref[:, at * quarter : (at + 1) * quarter] = dot(pick, pot_ref[...])

    for at in range(FG // LOCAL // 2):
        span = slice(at * LANES, (at + 1) * LANES)
        grid_vals = dot(after_y_ref[half, :, span], fwd_z) * (4.0 / FG**1.5)
        pot = pots_ref[:, at * 2 * LANES : (at + 1) * 2 * LANES]
        parts = [*spread_parts(pot[:, :LANES]), *spread_parts(pot[:, LANES:])]
        pots = jnp.concatenate([jnp.concatenate(parts, axis=1)] * LOCAL, axis=0)
        back_ref[:, span] = dot_t((grid_vals * pots).astype(BF16), fwd_z).astype(BF16)


def near_kernel(
    near_at_ref, after_y_ref, pot_ref, big_y_ref, fwd_z_ref, sum_ref, back_ref, pots_ref
):
    near = near_at_ref[0]
    weigh_half(near, after_y_ref, pot_ref, fwd_z_ref, back_ref, pots_ref)
    block_n = 2 * LANES
    for start in range(0, HB * 2 * QB, block_n):
        span = slice(start, start + block_n)
        sum_ref[:, span] = dot_t(back_ref[...], big_y_ref[near, span, :])


def step_kernel(
    near_at_ref, after_y_ref, pot_ref, big_y_ref, fwd_z_ref, sum_ref, bands_ref, back_x_ref,
    send_ref, stepped_ref, sent_ref, stack_ref, back_ref, pots_ref,
):
    far = 1 - near_at_ref[0]
    weigh_half(far, after_y_ref, pot_ref, fwd_z_ref, back_ref, pots_ref)
    rows_n = LOCAL * FG
    half_n = LOCAL * HB
    block_n = 2 * LANES
    for start in range(0, HB * 2 * QB, block_n):
        span = slice(start, start + block_n)
        block = sum_ref[:, span] + dot_t(back_ref[...], big_y_ref[far, span, :])
        stack_ref[:rows_n, span] = block.astype(BF16)
        for low in range(start, start + block_n, LANES):
            turned = times_i(block[:, low - start : low - start + LANES])
            stack_ref[rows_n:, low : low + LANES] = turned.astype(BF16)
        image = dot(back_x_ref[...], stack_ref[:, span]) * (0.25 / FG**1.5)
        shape = (half_n, block_n)
        row, lane = iota(shape, 0), iota(shape, 1) + start
        mx, my = row % HB - HB // 2, lane // (2 * QB) - HB // 2
        mz = lane % QB - QB // 2
        kinetic = (mx * mx + my * my + mz * mz).astype(F32) * (16.0 / FG**2)
        bands = bands_ref[:, span].astype(F32)
        stepped_ref[:, span] = (bands - STEP_TAU * (kinetic * bands + image)).astype(BF16)

    half_w = HB * QB
    halves_of = jnp.concatenate([stepped_ref[:, :half_w], stepped_ref[:, half_w:]], axis=0)
    sent_ref[...] = dot(send_ref[...], halves_of).astype(BF16)


def image_kernel(stepped_ref, fwd_x_ref, image_ref, stack_ref):
    half_n = LOCAL * HB
    stack_ref[:half_n, :] = stepped_ref[...]
    for start in range(0, HB * 2 * QB, LANES):
        block = stepped_ref[:, start : start + LANES].astype(F32)
        stack_ref[half_n:, start : start + LANES] = times_i(block).astype(BF16)
    coefs = HB * 2 * QB
    image_ref[:, :coefs] = dot(fwd_x_ref[...], stack_ref[...]).astype(BF16)
    image_ref[:, coefs:] = jnp.zeros((2 * NB, NB), BF16)


def gram_kernel(received_ref, image_any, out_any, stepped_ref, conj_ref, extra_ref, sem):
    coefs = HB * 2 * QB
    half_w = coefs // 2
    shape = (NB, 2 * NB)
    row, col = iota(shape, 0), iota(shape, 1)
    at = row // LOCAL * 2 * LOCAL + row % LOCAL
    picks = [onehot(col == at + half * LOCAL) for half in (0, 1)]
    for half in (0, 1):
        rows = dot(picks[half], received_ref[...])
        stepped_ref[:, half * half_w : (half + 1) * half_w] = rows.astype(BF16)
        for start in range(0, half_w, LANES):
            block = -times_i(rows[:, start : start + LANES])
            conj_ref[:, half * half_w + start : half * half_w + start + LANES] = block.astype(BF16)
    stepped = stepped_ref[...]
    gram_re = dot_t(stepped, stepped)
    gram_im = dot_t(stepped, conj_ref[...])
    shape = (NB, NB)
    gram = jnp.where(iota(shape, 0) >= iota(shape, 1), gram_re, gram_im) * (1.0 / COEF)
    upper, lower = halves(gram)
    shape = (2 * NB, NB)
    row, col = iota(shape, 0), iota(shape, 1)
    at = col // LOCAL * 2 * LOCAL + col % LOCAL
    spread = dot(onehot(row == at), upper) + dot(onehot(row == at + LOCAL), lower)
    extra_ref[...] = spread.astype(BF16)
    extra_copy = pltpu.make_async_copy(extra_ref, out_any.at[:, coefs:], sem)
    extra_copy.start()
    extra_copy.wait()


def sum_kernel(parts_ref, out_ref):
    parts = parts_ref[:, HB * 2 * QB :].astype(F32).reshape(HB, 2 * LOCAL, NB).sum(axis=0)
    whole = parts + pltpu.roll(parts, LOCAL, 0)
    out_ref[...] = jnp.broadcast_to(whole[None], (NB // 8, 8, NB)).reshape(NB, NB)


def complex_mul(left, right):
    turned = jnp.concatenate([-left[NB:], left[:NB]], axis=0)
    left_hi, left_lo = halves(jnp.concatenate([left, turned], axis=1))
    right_hi, right_lo = halves(right)
    first = dot(left_hi, jnp.concatenate([right_hi, right_lo], axis=1))
    return first[:, :NB] + (first[:, NB:] + dot(left_lo, right_hi))


def newton_kernel(gram_ref, stepped_ref, phi_ref, inv_ref, stack_ref):
    packed = gram_ref[...]
    flipped = packed.T
    shape = (NB, NB)
    row, col = iota(shape, 0), iota(shape, 1)
    gram_re = jnp.where(row >= col, packed, flipped)
    gram_im = jnp.where(row < col, packed, jnp.where(row > col, -flipped, 0.0))
    total = jnp.sum(gram_re * gram_re + gram_im * gram_im, axis=1, keepdims=True)
    scale = jnp.sqrt(jnp.sum(total, axis=0, keepdims=True) + NORM_EPS)
    eye = (row == col).astype(F32)
    identity = jnp.concatenate([eye, jnp.zeros(shape, F32)], axis=0)
    iter_y = jnp.concatenate([gram_re, gram_im], axis=0) / scale
    iter_z = identity
    for at in range(NEWTON):
        product = complex_mul(iter_z, iter_y) if at else iter_y
        factor = 1.5 * identity - 0.5 * product
        if at < NEWTON - 1:
            iter_y = complex_mul(iter_y, factor)
        iter_z = complex_mul(factor, iter_z) if at else factor
    inverse = iter_z / jnp.sqrt(scale)
    inv_re, inv_im = inverse[:NB].T, inverse[NB:].T
    re_hi, re_lo = halves(inv_re)
    im_hi, im_lo = halves(inv_im)
    inv_ref[...] = jnp.concatenate([re_hi, im_hi, re_lo, im_lo], axis=0)
    stack_ref[:NB, :] = stepped_ref[...]
    for start in range(0, HB * 2 * QB, LANES):
        block = stepped_ref[:, start : start + LANES].astype(F32)
        stack_ref[NB:, start : start + LANES] = times_i(block).astype(BF16)
    left = jnp.concatenate(
        [jnp.concatenate([re_hi, im_hi], axis=1), jnp.concatenate([re_lo, im_lo], axis=1)], axis=0
    )
    both = dot(left, stack_ref[...])
    phi = (both[:NB] + both[NB:]).astype(BF16)
    half_w = HB * QB
    shape = (2 * NB, NB)
    row, col = iota(shape, 0), iota(shape, 1)
    same = row // (2 * LOCAL) * LOCAL + row % LOCAL == col
    picks = [onehot(same & (row // LOCAL % 2 == half)) for half in (0, 1)]
    sent = dot(picks[0], phi[:, :half_w]) + dot(picks[1], phi[:, half_w:])
    phi_ref[...] = sent.astype(BF16)


def density_kernel(
    place_ref, own_ref, image_ref, inv_ref, big_y_ref, fwd_z_ref, tile_ref,
    out_ref, stack_ref, phi_ref, after_y_ref, dens_ref,
):
    rows_n = 2 * NB
    shape = (NB, 2 * rows_n)
    row, col = iota(shape, 0), iota(shape, 1)
    inner = col % rows_n
    picks = (inner // 8 * LOCAL + inner % LOCAL == row) & (inner // LOCAL % 2 == col // rows_n)
    spread = dot(inv_ref[...], picks.astype(F32).astype(BF16)).astype(BF16)
    stack_ref[:rows_n, :] = image_ref[:, : HB * 2 * QB]
    for start in range(0, HB * 2 * QB, LANES):
        block = image_ref[:, start : start + LANES].astype(F32)
        stack_ref[rows_n:, start : start + LANES] = times_i(block).astype(BF16)
    left = jnp.concatenate(
        [
            jnp.concatenate(
                [
                    spread[base : base + NB, at * rows_n : (at + 1) * rows_n]
                    for base in (low, low + NB)
                ],
                axis=1,
            )
            for low in (0, 2 * NB)
            for at in (0, 1)
        ],
        axis=0,
    )
    both = dot(left, stack_ref[...])
    phi_ref[...] = (both[:rows_n] + both[rows_n:]).astype(BF16)
    half_w = FG * QB
    for half in (0, 1):
        for start in range(0, half_w, 512):
            block = dot(phi_ref[...], big_y_ref[half, :, start : start + 512])
            for low in (0, 256):
                at = (start + low) * 2 + half * 256
                after_y_ref[:, at : at + 256] = block[:, low : low + 256].astype(BF16)

    low = iota((1, LANES), 1) < FG

    @pl.loop(0, FG // LOCAL, unroll=4)
    def _(at):
        span = pl.ds(pl.multiple_of(at * LANES, LANES), LANES)
        grid_vals = dot(after_y_ref[:, span], fwd_z_ref[...]) * (4.0 / FG**1.5)
        square = grid_vals * grid_vals
        sums = [
            jnp.sum(square[plane * NB : (plane + 1) * NB], axis=0, keepdims=True) * (2.0 / NB)
            for plane in (0, 1)
        ]
        for y_lo in range(LOCAL):
            parts = [s[:, y_lo * LANES : (y_lo + 1) * LANES] for s in sums]
            full = [p + pltpu.roll(p, FG, 1) for p in parts]
            dens_ref[pl.ds(at * LOCAL + y_lo, 1), :] = jnp.where(low, full[0], full[1])

    own = own_ref[0]
    own_y, own_z = place_ref[own, 1], place_ref[own, 2]
    sign = place_ref[own, 0].astype(F32)
    dens = (dens_ref[...] * sign).astype(BF16)
    shape = (LANES, LANES)
    row, col = iota(shape, 0), iota(shape, 1)
    same_plane = row // FG == col // FG
    rows_shape = (FG, FG)
    rows_row, rows_col = iota(rows_shape, 0), iota(rows_shape, 1)
    tiles = [jnp.concatenate(halves(tile_ref[plane]), axis=0) for plane in (0, 1)]
    for to in range(FRAGS):
        shift_y = place_ref[to, 1] - own_y + GY
        shift_z = place_ref[to, 2] - own_z + GZ
        cols = same_plane & ((col % FG + shift_z) % GZ == row % FG)
        moved = dot(dens, cols.astype(F32).astype(BF16)).astype(BF16)
        rows = (rows_row + shift_y) % GY == rows_col
        out_ref[to, :FG, :] = dot(rows.astype(F32).astype(BF16), moved).astype(BF16)
        to_z = place_ref[to, 2]
        tile = jnp.zeros((2 * 8, LANES), F32)
        for plane in (0, 1):
            cols = onehot((col // FG == plane) & ((col % FG + to_z) % GZ == row))
            tile += dot(tiles[plane], cols)
        out_ref[to, FG:, :] = tile.astype(BF16)


def last_kernel(place_ref, own_ref, pieces_ref, out_ref, total_ref):
    own = own_ref[0]
    own_y = place_ref[own, 1]
    patched = jnp.zeros((FG, LANES), F32)
    for at in range(FRAGS):
        patched += pieces_ref[at, :FG, :].astype(F32)
    rows = onehot((iota((FG, GY), 0) + own_y) % GY == iota((FG, GY), 1))
    tiles = pieces_ref[:, FG:, :].astype(F32)
    total = jnp.zeros((FG, LANES), F32)
    for part in (0, 1):
        tile = tiles[:, part * 8 : (part + 1) * 8, :].reshape(GY, LANES)
        total += dot(rows, tile.astype(BF16))
    power = jnp.exp(jnp.log(patched * patched + SOFTEN) * (-1.0 / 3.0))
    total_ref[...] = total - SLATER * patched * power
    even = total_ref[pl.ds(0, FG // 2, stride=2), :]
    odd = total_ref[pl.ds(1, FG // 2, stride=2), :]
    low = iota(even.shape, 1) < FG
    planes = [jnp.where(low, even, pltpu.roll(odd, FG, 1)), jnp.where(low, pltpu.roll(even, FG, 1), odd)]
    for plane in (0, 1):
        for at in range(FG // 2):
            out_ref[plane : plane + 1, at * LANES : (at + 1) * LANES] = planes[plane][at : at + 1]


VM = pl.BlockSpec(memory_space=pltpu.VMEM)
SM = pl.BlockSpec(memory_space=pltpu.SMEM)
ANY = pl.BlockSpec(memory_space=pl.ANY)
HBM = pl.BlockSpec(memory_space=pltpu.HBM)


def sds(shape, dtype):
    return jax.ShapeDtypeStruct(shape, dtype)


def call(kernel, outs, in_specs, scratch, flops, moved, name, copies=0, out_specs=None, aliases=None):
    return pl.pallas_call(
        kernel,
        out_shape=outs,
        in_specs=in_specs,
        out_specs=out_specs or jax.tree.map(lambda _: VM, outs),
        scratch_shapes=[pltpu.VMEM(s, d) for s, d in scratch]
        + ([pltpu.SemaphoreType.DMA((copies,) if copies > 1 else ())] if copies else []),
        input_output_aliases=aliases or {},
        cost_estimate=pl.CostEstimate(flops=flops, bytes_accessed=moved, transcendentals=0),
        compiler_params=pltpu.CompilerParams(vmem_limit_bytes=GRANT.get(name, 8) << 20),
    )


GRANT = {"forward": 16, "near": 8, "step": 10, "density": 24}


def stages():
    coefs = HB * 2 * QB
    width = FG * 2 * QB
    mega = 1 << 20
    forward = call(
        forward_kernel,
        (sds((2, coefs, width // 2), BF16), sds((2, LOCAL * FG, width // 2), BF16)),
        [VM] * 3,
        [((2 * HB, width), F32), ((2 * LOCAL * HB, coefs), BF16)],
        2 * 10**9, 6 * mega, "forward",
    )
    weigh = [
        ((LOCAL * FG, width // 2), BF16),
        ((FG, FG * FG // 2), F32),
    ]
    near = call(
        near_kernel, sds((LOCAL * FG, coefs), F32), [SM] + [VM] * 4, weigh,
        2 * 10**9, 4 * mega, "near",
    )
    step = call(
        step_kernel,
        (sds((LOCAL * HB, coefs), BF16), sds((2 * NB, coefs // 2), BF16)),
        [SM] + [VM] * 8,
        [((2 * LOCAL * FG, coefs), BF16)] + weigh,
        2 * 10**9, 4 * mega, "step",
    )
    image = call(
        image_kernel, sds((LOCAL * FG, coefs + NB), BF16), [VM] * 2,
        [((2 * LOCAL * HB, coefs), BF16)], 10**8, mega, "image",
    )
    gram = call(
        gram_kernel,
        (sds((2 * NB, coefs + NB), BF16), sds((NB, coefs), BF16)),
        [VM, ANY],
        [((NB, coefs), BF16), ((2 * NB, NB), BF16)],
        2 * 10**8, 2 * mega, "gram", 1, (ANY, VM), {1: 0},
    )
    total = call(
        sum_kernel, sds((NB, NB), F32), [VM], [], 10**6, mega // 8, "total",
    )
    newton = call(
        newton_kernel,
        (sds((2 * NB, coefs // 2), BF16), sds((4 * NB, NB), BF16)),
        [VM] * 2,
        [((2 * NB, coefs), BF16)],
        10**9, mega, "newton",
    )
    density = call(
        density_kernel,
        sds((FRAGS, FG + 16, LANES), BF16),
        [SM, SM] + [VM] * 5,
        [
            ((4 * NB, coefs), BF16),
            ((2 * NB, coefs), BF16),
            ((2 * NB, width), BF16),
            ((FG, LANES), F32),
        ],
        4 * 10**9, 6 * mega, "density",
    )
    last = call(
        last_kernel, sds((2, FG * FG), F32), [SM, SM, VM], [((FG, LANES), F32)],
        10**7, mega // 2, "last",
    )
    return forward, near, step, image, gram, total, newton, density, last


def exchange(values, axis):
    return lax.all_to_all(values, axis, split_axis=0, concat_axis=0, tiled=True)


def per_device(bands_in, potential_in, hartree, patch_list):
    fwd_x, fwd_x_send, back_x, fwd_y, fwd_z, send = dft_tables()
    forward, near, step, image, gram, total, newton, density, last = stages()
    coefs = HB * 2 * QB
    groups = lax.axis_size("band")
    chips = groups // 2
    planes = FG // groups
    own = lax.axis_index("frag").astype(jnp.int32).reshape(1)
    near_at = (lax.axis_index("band") & 1).astype(jnp.int32).reshape(1)

    pot = potential_in.astype(BF16).reshape(planes * 4, FG * FG // 4)
    pot = jnp.stack([pot[:, : FG * FG // 8], pot[:, FG * FG // 8 :]])[None]
    pot = jnp.broadcast_to(pot, (chips, *pot.shape[1:])).reshape(groups, *pot.shape[2:])
    pot_near = exchange(pot, "band").reshape(4 * FG, FG * FG // 8)
    pot_far = lax.ppermute(pot_near, "band", [(i, i ^ 1) for i in range(groups)])
    bands = bands_in.reshape(LOCAL * HB, coefs)
    big_y, after_y = forward(bands, fwd_x, fwd_y)
    near_rows = near(near_at, after_y, pot_near, big_y, fwd_z)
    stepped_own, stepped_send = step(
        near_at, after_y, pot_far, big_y, fwd_z, near_rows, bands, back_x, send
    )
    received = exchange(stepped_send.reshape(groups, 2 * LOCAL, coefs // 2), "band")
    image_send = image(stepped_own, fwd_x_send)
    parts, stepped = gram(received.reshape(2 * NB, coefs // 2), image_send)
    parts = exchange(parts.reshape(groups, planes * LOCAL, -1), "band").reshape(2 * NB, -1)
    whole = exchange(total(parts).reshape(groups, LOCAL, NB), "band").reshape(NB, NB)
    phi, inverse = newton(whole, stepped)
    phi_local = exchange(phi.reshape(groups, 2 * LOCAL, coefs // 2), "band")
    pieces = density(patch_list, own, parts, inverse, big_y, fwd_z, hartree)
    pieces, phi_local = lax.optimization_barrier((pieces, phi_local))
    back = last(patch_list, own, exchange(pieces, "frag")).reshape(1, planes, FG * FG)
    bands_out = phi_local.reshape(groups, 2, LOCAL, coefs // 2).transpose(2, 0, 1, 3)
    bands_out = bands_out.astype(F32).reshape(1, LOCAL, HB * coefs)
    return (bands_out, back)


def solution(mesh):
    in_specs = (P("frag", "band", None), P("frag", "band", None), P("band", "frag", None), P())
    out_specs = (P("frag", "band", None), P("frag", "band", None))

    return jax.shard_map(
        per_device, mesh=mesh, in_specs=in_specs, out_specs=out_specs, check_vma=False
    )
```

```python
import math

import numpy as np

import jax
import jax.numpy as jnp
from jax import lax
from jax.experimental import pallas as pl
from jax.experimental.pallas import tpu as pltpu
from jax.sharding import PartitionSpec as P


FG = 64
NB = 128
NEWTON = 6
COEF = 16384
FRAGS = 16
GY = 128
GZ = 128
HB = FG // 2
QB = FG // 4

SLATER = 0.9847
SOFTEN = 0.25
STEP_TAU = 0.5
NORM_EPS = 1e-06

F32 = jnp.float32
BF16 = jnp.bfloat16
LOCAL = 4
LANES = 128


def dft_tables():
    places = np.arange(FG)
    freq_xy = np.arange(HB) - HB // 2
    freq_z = np.arange(QB) - QB // 2
    turn_xy = 2.0 * math.pi / FG * ((places[:, None] * freq_xy[None, :]) % FG)
    turn_z = 2.0 * math.pi / FG * ((freq_z[:, None] * places[None, :]) % FG)
    cos_xy, sin_xy = np.cos(turn_xy), np.sin(turn_xy)
    cos_z, sin_z = np.cos(turn_z), np.sin(turn_z)
    same = np.eye(LOCAL)
    fwd_x = np.stack([np.einsum("ab,xk->axbk", same, t) for t in (cos_xy, sin_xy)], axis=2)
    fwd_x = fwd_x.reshape(LOCAL * FG, 2 * LOCAL * HB)
    fwd_x_send = fwd_x.reshape(LOCAL, FG // 2, 2, -1).transpose(1, 2, 0, 3)
    fwd_x_send = fwd_x_send.reshape(LOCAL * FG, -1)
    back_x = np.stack([np.einsum("ab,xk->akbx", same, t) for t in (cos_xy, -sin_xy)], axis=0)
    back_x = back_x.reshape(2 * LOCAL * HB, LOCAL * FG)
    fwd_y = np.stack(
        [np.stack([cos_xy.T, sin_xy.T], axis=2), np.stack([-sin_xy.T, cos_xy.T], axis=2)], axis=1
    ).reshape(2 * HB, 2 * FG)
    one_z = np.block([[cos_z, sin_z], [-sin_z, cos_z]])
    fwd_z = np.einsum("ab,kz->akbz", same, one_z).reshape(LOCAL * 2 * QB, LOCAL * 2 * FG)
    send = np.einsum("gh,ab,kl->kgahbl", np.eye(2), same, np.eye(HB))
    send = send.reshape(2 * LOCAL * HB, 2 * LOCAL * HB)
    return tuple(
        jnp.asarray(t, dtype=F32).astype(BF16)
        for t in (fwd_x, fwd_x_send, back_x, fwd_y, fwd_z, send)
    )


def iota(shape, axis):
    return lax.broadcasted_iota(jnp.int32, shape, axis)


def dot(left, right):
    return jnp.dot(left, right, preferred_element_type=F32)


def dot_t(left, right):
    return lax.dot_general(left, right, (((1,), (1,)), ((), ())), preferred_element_type=F32)


def onehot(matches):
    return matches.astype(F32).astype(BF16)


def times_i(block):
    first = iota(block.shape, 1) % (2 * QB) < QB
    ahead = pltpu.roll(block, LANES - QB, 1)
    behind = pltpu.roll(block, QB, 1)
    return jnp.where(first, -ahead, behind)


def halves(values):
    upper = values.astype(BF16)
    return upper, (values - upper.astype(F32)).astype(BF16)


def forward_kernel(bands_ref, fwd_x_ref, fwd_y_ref, big_y_ref, out_ref, rows_ref, stack_ref):
    width = FG * 2 * QB
    half_w = width // 2
    spread = onehot(iota((2 * FG, width), 1) // QB == iota((2 * FG, width), 0))
    rows_ref[...] = dot(fwd_y_ref[...], spread)
    same = iota((QB, width), 1) % QB == iota((QB, width), 0)

    @pl.loop(0, 2 * HB, unroll=8)
    def _(row):
        line = jnp.broadcast_to(rows_ref[pl.ds(row, 1), :], (QB, width))
        start = pl.multiple_of(row * QB, QB)
        lines = jnp.where(same, line, 0.0).astype(BF16)
        for at in range(8):
            block = lines[:, at * 256 : (at + 1) * 256]
            big_y_ref[at % 2, pl.ds(start, QB), at // 2 * 256 : (at // 2 + 1) * 256] = block

    rows_n = LOCAL * HB
    stack_ref[:rows_n, :] = bands_ref[...]
    for start in range(0, HB * 2 * QB, LANES):
        block = bands_ref[:, start : start + LANES].astype(F32)
        stack_ref[rows_n:, start : start + LANES] = times_i(block).astype(BF16)
    after_x = dot(fwd_x_ref[...], stack_ref[...]).astype(BF16)
    for half in (0, 1):
        for start in range(0, half_w, 512):
            span = slice(start, start + 512)
            out_ref[half, :, span] = dot(after_x, big_y_ref[half, :, span]).astype(BF16)


def spread_parts(pair):
    low = iota(pair.shape, 1) < FG
    turned = pltpu.roll(pair, FG, 1)
    return jnp.where(low, pair, turned), jnp.where(low, turned, pair)


def weigh_half(half, after_y_ref, pot_ref, fwd_z_ref, back_ref, pots_ref):
    fwd_z = fwd_z_ref[...]
    quarter = FG * FG // 8
    pick_shape = (FG, LOCAL * FG)
    for at in range(4):
        pick = onehot(iota(pick_shape, 0) * 4 + at == iota(pick_shape, 1))
        pots_ref[:, at * quarter : (at + 1) * quarter] = dot(pick, pot_ref[...])

    for at in range(FG // LOCAL // 2):
        span = slice(at * LANES, (at + 1) * LANES)
        grid_vals = dot(after_y_ref[half, :, span], fwd_z) * (4.0 / FG**1.5)
        pot = pots_ref[:, at * 2 * LANES : (at + 1) * 2 * LANES]
        parts = [*spread_parts(pot[:, :LANES]), *spread_parts(pot[:, LANES:])]
        pots = jnp.concatenate([jnp.concatenate(parts, axis=1)] * LOCAL, axis=0)
        back_ref[:, span] = dot_t((grid_vals * pots).astype(BF16), fwd_z).astype(BF16)


def near_kernel(
    near_at_ref, after_y_ref, pot_ref, big_y_ref, fwd_z_ref, sum_ref, back_ref, pots_ref
):
    near = near_at_ref[0]
    weigh_half(near, after_y_ref, pot_ref, fwd_z_ref, back_ref, pots_ref)
    block_n = 2 * LANES
    for start in range(0, HB * 2 * QB, block_n):
        span = slice(start, start + block_n)
        sum_ref[:, span] = dot_t(back_ref[...], big_y_ref[near, span, :])


def step_kernel(
    near_at_ref, after_y_ref, pot_ref, big_y_ref, fwd_z_ref, sum_ref, bands_ref, back_x_ref,
    send_ref, stepped_ref, sent_ref, back_ref, pots_ref,
):
    far = 1 - near_at_ref[0]
    weigh_half(far, after_y_ref, pot_ref, fwd_z_ref, back_ref, pots_ref)
    half_n = LOCAL * HB
    block_n = 2 * LANES
    for start in range(0, HB * 2 * QB, block_n):
        span = slice(start, start + block_n)
        block = sum_ref[:, span] + dot_t(back_ref[...], big_y_ref[far, span, :])
        both = dot(back_x_ref[...], block.astype(BF16))
        turned = [times_i(both[half_n:, low : low + LANES]) for low in (0, LANES)]
        image = (both[:half_n] + jnp.concatenate(turned, axis=1)) * (0.25 / FG**1.5)
        shape = (half_n, block_n)
        row, lane = iota(shape, 0), iota(shape, 1) + start
        mx, my = row % HB - HB // 2, lane // (2 * QB) - HB // 2
        mz = lane % QB - QB // 2
        kinetic = (mx * mx + my * my + mz * mz).astype(F32) * (16.0 / FG**2)
        bands = bands_ref[:, span].astype(F32)
        stepped_ref[:, span] = (bands - STEP_TAU * (kinetic * bands + image)).astype(BF16)

    half_w = HB * QB
    halves_of = jnp.concatenate([stepped_ref[:, :half_w], stepped_ref[:, half_w:]], axis=0)
    sent_ref[...] = dot(send_ref[...], halves_of).astype(BF16)


def image_kernel(stepped_ref, fwd_x_ref, image_ref, stack_ref):
    half_n = LOCAL * HB
    stack_ref[:half_n, :] = stepped_ref[...]
    for start in range(0, HB * 2 * QB, LANES):
        block = stepped_ref[:, start : start + LANES].astype(F32)
        stack_ref[half_n:, start : start + LANES] = times_i(block).astype(BF16)
    coefs = HB * 2 * QB
    image_ref[:, :coefs] = dot(fwd_x_ref[...], stack_ref[...]).astype(BF16)
    image_ref[:, coefs:] = jnp.zeros((2 * NB, NB), BF16)


def gram_kernel(received_ref, image_any, out_any, stepped_ref, conj_ref, extra_ref, sem):
    coefs = HB * 2 * QB
    half_w = coefs // 2
    shape = (NB, 2 * NB)
    row, col = iota(shape, 0), iota(shape, 1)
    at = row // LOCAL * 2 * LOCAL + row % LOCAL
    picks = [onehot(col == at + half * LOCAL) for half in (0, 1)]
    for half in (0, 1):
        rows = dot(picks[half], received_ref[...])
        stepped_ref[:, half * half_w : (half + 1) * half_w] = rows.astype(BF16)
        for start in range(0, half_w, LANES):
            block = -times_i(rows[:, start : start + LANES])
            conj_ref[:, half * half_w + start : half * half_w + start + LANES] = block.astype(BF16)
    stepped = stepped_ref[...]
    gram_re = dot_t(stepped, stepped)
    gram_im = dot_t(stepped, conj_ref[...])
    shape = (NB, NB)
    gram = jnp.where(iota(shape, 0) >= iota(shape, 1), gram_re, gram_im) * (1.0 / COEF)
    upper, lower = halves(gram)
    shape = (2 * NB, NB)
    row, col = iota(shape, 0), iota(shape, 1)
    at = col // LOCAL * 2 * LOCAL + col % LOCAL
    spread = dot(onehot(row == at), upper) + dot(onehot(row == at + LOCAL), lower)
    extra_ref[...] = spread.astype(BF16)
    extra_copy = pltpu.make_async_copy(extra_ref, out_any.at[:, coefs:], sem)
    extra_copy.start()
    extra_copy.wait()


def sum_kernel(parts_ref, out_ref):
    parts = parts_ref[:, HB * 2 * QB :].astype(F32).reshape(HB, 2 * LOCAL, NB).sum(axis=0)
    whole = parts + pltpu.roll(parts, LOCAL, 0)
    out_ref[...] = jnp.broadcast_to(whole[None], (NB // 8, 8, NB)).reshape(NB, NB)


def complex_mul(left, right):
    turned = jnp.concatenate([-left[NB:], left[:NB]], axis=0)
    left_hi, left_lo = halves(jnp.concatenate([left, turned], axis=1))
    right_hi, right_lo = halves(right)
    first = dot(left_hi, jnp.concatenate([right_hi, right_lo], axis=1))
    return first[:, :NB] + (first[:, NB:] + dot(left_lo, right_hi))


def newton_kernel(gram_ref, stepped_ref, phi_ref, inv_ref, stack_ref):
    packed = gram_ref[...]
    flipped = packed.T
    shape = (NB, NB)
    row, col = iota(shape, 0), iota(shape, 1)
    gram_re = jnp.where(row >= col, packed, flipped)
    gram_im = jnp.where(row < col, packed, jnp.where(row > col, -flipped, 0.0))
    total = jnp.sum(gram_re * gram_re + gram_im * gram_im, axis=1, keepdims=True)
    scale = jnp.sqrt(jnp.sum(total, axis=0, keepdims=True) + NORM_EPS)
    eye = (row == col).astype(F32)
    identity = jnp.concatenate([eye, jnp.zeros(shape, F32)], axis=0)
    iter_y = jnp.concatenate([gram_re, gram_im], axis=0) / scale
    iter_z = identity
    for at in range(NEWTON):
        product = complex_mul(iter_z, iter_y) if at else iter_y
        factor = 1.5 * identity - 0.5 * product
        if at < NEWTON - 1:
            iter_y = complex_mul(iter_y, factor)
        iter_z = complex_mul(factor, iter_z) if at else factor
    inverse = iter_z / jnp.sqrt(scale)
    inv_re, inv_im = inverse[:NB].T, inverse[NB:].T
    re_hi, re_lo = halves(inv_re)
    im_hi, im_lo = halves(inv_im)
    inv_ref[...] = jnp.concatenate([re_hi, im_hi, re_lo, im_lo], axis=0)
    stack_ref[:NB, :] = stepped_ref[...]
    for start in range(0, HB * 2 * QB, LANES):
        block = stepped_ref[:, start : start + LANES].astype(F32)
        stack_ref[NB:, start : start + LANES] = times_i(block).astype(BF16)
    left = jnp.concatenate(
        [jnp.concatenate([re_hi, im_hi], axis=1), jnp.concatenate([re_lo, im_lo], axis=1)], axis=0
    )
    both = dot(left, stack_ref[...])
    phi = (both[:NB] + both[NB:]).astype(BF16)
    half_w = HB * QB
    shape = (2 * NB, NB)
    row, col = iota(shape, 0), iota(shape, 1)
    same = row // (2 * LOCAL) * LOCAL + row % LOCAL == col
    picks = [onehot(same & (row // LOCAL % 2 == half)) for half in (0, 1)]
    sent = dot(picks[0], phi[:, :half_w]) + dot(picks[1], phi[:, half_w:])
    phi_ref[...] = sent.astype(BF16)


def density_kernel(
    place_ref, own_ref, image_ref, inv_ref, big_y_ref, fwd_z_ref, tile_ref,
    out_ref, stack_ref, phi_ref, after_y_ref, dens_ref,
):
    rows_n = 2 * NB
    shape = (NB, 2 * rows_n)
    row, col = iota(shape, 0), iota(shape, 1)
    inner = col % rows_n
    picks = (inner // 8 * LOCAL + inner % LOCAL == row) & (inner // LOCAL % 2 == col // rows_n)
    spread = dot(inv_ref[...], picks.astype(F32).astype(BF16)).astype(BF16)
    stack_ref[:rows_n, :] = image_ref[:, : HB * 2 * QB]
    for start in range(0, HB * 2 * QB, LANES):
        block = image_ref[:, start : start + LANES].astype(F32)
        stack_ref[rows_n:, start : start + LANES] = times_i(block).astype(BF16)
    left = jnp.concatenate(
        [
            jnp.concatenate(
                [
                    spread[base : base + NB, at * rows_n : (at + 1) * rows_n]
                    for base in (low, low + NB)
                ],
                axis=1,
            )
            for low in (0, 2 * NB)
            for at in (0, 1)
        ],
        axis=0,
    )
    both = dot(left, stack_ref[...])
    phi_ref[...] = (both[:rows_n] + both[rows_n:]).astype(BF16)
    half_w = FG * QB
    for half in (0, 1):
        for start in range(0, half_w, 512):
            block = dot(phi_ref[...], big_y_ref[half, :, start : start + 512])
            for low in (0, 256):
                at = (start + low) * 2 + half * 256
                after_y_ref[:, at : at + 256] = block[:, low : low + 256].astype(BF16)

    low = iota((1, LANES), 1) < FG

    @pl.loop(0, FG // LOCAL, unroll=4)
    def _(at):
        span = pl.ds(pl.multiple_of(at * LANES, LANES), LANES)
        grid_vals = dot(after_y_ref[:, span], fwd_z_ref[...]) * (4.0 / FG**1.5)
        square = grid_vals * grid_vals
        sums = [
            jnp.sum(square[plane * NB : (plane + 1) * NB], axis=0, keepdims=True) * (2.0 / NB)
            for plane in (0, 1)
        ]
        for y_lo in range(LOCAL):
            parts = [s[:, y_lo * LANES : (y_lo + 1) * LANES] for s in sums]
            full = [p + pltpu.roll(p, FG, 1) for p in parts]
            dens_ref[pl.ds(at * LOCAL + y_lo, 1), :] = jnp.where(low, full[0], full[1])

    own = own_ref[0]
    own_y, own_z = place_ref[own, 1], place_ref[own, 2]
    sign = place_ref[own, 0].astype(F32)
    dens = (dens_ref[...] * sign).astype(BF16)
    shape = (LANES, LANES)
    row, col = iota(shape, 0), iota(shape, 1)
    same_plane = row // FG == col // FG
    rows_shape = (FG, FG)
    rows_row, rows_col = iota(rows_shape, 0), iota(rows_shape, 1)
    tiles = [jnp.concatenate(halves(tile_ref[plane]), axis=0) for plane in (0, 1)]
    for to in range(FRAGS):
        shift_y = place_ref[to, 1] - own_y + GY
        shift_z = place_ref[to, 2] - own_z + GZ
        cols = same_plane & ((col % FG + shift_z) % GZ == row % FG)
        moved = dot(dens, cols.astype(F32).astype(BF16)).astype(BF16)
        rows = (rows_row + shift_y) % GY == rows_col
        out_ref[to, :FG, :] = dot(rows.astype(F32).astype(BF16), moved).astype(BF16)
        to_z = place_ref[to, 2]
        tile = jnp.zeros((2 * 8, LANES), F32)
        for plane in (0, 1):
            cols = onehot((col // FG == plane) & ((col % FG + to_z) % GZ == row))
            tile += dot(tiles[plane], cols)
        out_ref[to, FG:, :] = tile.astype(BF16)


def last_kernel(place_ref, own_ref, pieces_ref, out_ref, total_ref):
    own = own_ref[0]
    own_y = place_ref[own, 1]
    patched = jnp.zeros((FG, LANES), F32)
    for at in range(FRAGS):
        patched += pieces_ref[at, :FG, :].astype(F32)
    rows = onehot((iota((FG, GY), 0) + own_y) % GY == iota((FG, GY), 1))
    tiles = pieces_ref[:, FG:, :].astype(F32)
    total = jnp.zeros((FG, LANES), F32)
    for part in (0, 1):
        tile = tiles[:, part * 8 : (part + 1) * 8, :].reshape(GY, LANES)
        total += dot(rows, tile.astype(BF16))
    power = jnp.exp(jnp.log(patched * patched + SOFTEN) * (-1.0 / 3.0))
    total_ref[...] = total - SLATER * patched * power
    even = total_ref[pl.ds(0, FG // 2, stride=2), :]
    odd = total_ref[pl.ds(1, FG // 2, stride=2), :]
    low = iota(even.shape, 1) < FG
    planes = [jnp.where(low, even, pltpu.roll(odd, FG, 1)), jnp.where(low, pltpu.roll(even, FG, 1), odd)]
    for plane in (0, 1):
        for at in range(FG // 2):
            out_ref[plane : plane + 1, at * LANES : (at + 1) * LANES] = planes[plane][at : at + 1]


VM = pl.BlockSpec(memory_space=pltpu.VMEM)
SM = pl.BlockSpec(memory_space=pltpu.SMEM)
ANY = pl.BlockSpec(memory_space=pl.ANY)
HBM = pl.BlockSpec(memory_space=pltpu.HBM)


def sds(shape, dtype):
    return jax.ShapeDtypeStruct(shape, dtype)


def call(kernel, outs, in_specs, scratch, flops, moved, name, copies=0, out_specs=None, aliases=None):
    return pl.pallas_call(
        kernel,
        out_shape=outs,
        in_specs=in_specs,
        out_specs=out_specs or jax.tree.map(lambda _: VM, outs),
        scratch_shapes=[pltpu.VMEM(s, d) for s, d in scratch]
        + ([pltpu.SemaphoreType.DMA((copies,) if copies > 1 else ())] if copies else []),
        input_output_aliases=aliases or {},
        cost_estimate=pl.CostEstimate(flops=flops, bytes_accessed=moved, transcendentals=0),
        compiler_params=pltpu.CompilerParams(vmem_limit_bytes=GRANT.get(name, 8) << 20),
    )


GRANT = {"forward": 16, "near": 8, "step": 10, "density": 24}


def stages():
    coefs = HB * 2 * QB
    width = FG * 2 * QB
    mega = 1 << 20
    forward = call(
        forward_kernel,
        (sds((2, coefs, width // 2), BF16), sds((2, LOCAL * FG, width // 2), BF16)),
        [VM] * 3,
        [((2 * HB, width), F32), ((2 * LOCAL * HB, coefs), BF16)],
        2 * 10**9, 6 * mega, "forward",
    )
    weigh = [
        ((LOCAL * FG, width // 2), BF16),
        ((FG, FG * FG // 2), F32),
    ]
    near = call(
        near_kernel, sds((LOCAL * FG, coefs), F32), [SM] + [VM] * 4, weigh,
        2 * 10**9, 4 * mega, "near",
    )
    step = call(
        step_kernel,
        (sds((LOCAL * HB, coefs), BF16), sds((2 * NB, coefs // 2), BF16)),
        [SM] + [VM] * 8,
        weigh,
        2 * 10**9, 4 * mega, "step",
    )
    image = call(
        image_kernel, sds((LOCAL * FG, coefs + NB), BF16), [VM] * 2,
        [((2 * LOCAL * HB, coefs), BF16)], 10**8, mega, "image",
    )
    gram = call(
        gram_kernel,
        (sds((2 * NB, coefs + NB), BF16), sds((NB, coefs), BF16)),
        [VM, ANY],
        [((NB, coefs), BF16), ((2 * NB, NB), BF16)],
        2 * 10**8, 2 * mega, "gram", 1, (ANY, VM), {1: 0},
    )
    total = call(
        sum_kernel, sds((NB, NB), F32), [VM], [], 10**6, mega // 8, "total",
    )
    newton = call(
        newton_kernel,
        (sds((2 * NB, coefs // 2), BF16), sds((4 * NB, NB), BF16)),
        [VM] * 2,
        [((2 * NB, coefs), BF16)],
        10**9, mega, "newton",
    )
    density = call(
        density_kernel,
        sds((FRAGS, FG + 16, LANES), BF16),
        [SM, SM] + [VM] * 5,
        [
            ((4 * NB, coefs), BF16),
            ((2 * NB, coefs), BF16),
            ((2 * NB, width), BF16),
            ((FG, LANES), F32),
        ],
        4 * 10**9, 6 * mega, "density",
    )
    last = call(
        last_kernel, sds((2, FG * FG), F32), [SM, SM, VM], [((FG, LANES), F32)],
        10**7, mega // 2, "last",
    )
    return forward, near, step, image, gram, total, newton, density, last


def exchange(values, axis):
    return lax.all_to_all(values, axis, split_axis=0, concat_axis=0, tiled=True)


def per_device(bands_in, potential_in, hartree, patch_list):
    fwd_x, fwd_x_send, back_x, fwd_y, fwd_z, send = dft_tables()
    forward, near, step, image, gram, total, newton, density, last = stages()
    coefs = HB * 2 * QB
    groups = lax.axis_size("band")
    chips = groups // 2
    planes = FG // groups
    own = lax.axis_index("frag").astype(jnp.int32).reshape(1)
    near_at = (lax.axis_index("band") & 1).astype(jnp.int32).reshape(1)

    pot = potential_in.astype(BF16).reshape(planes * 4, FG * FG // 4)
    pot = jnp.stack([pot[:, : FG * FG // 8], pot[:, FG * FG // 8 :]])[None]
    pot = jnp.broadcast_to(pot, (chips, *pot.shape[1:])).reshape(groups, *pot.shape[2:])
    pot_near = exchange(pot, "band").reshape(4 * FG, FG * FG // 8)
    pot_far = lax.ppermute(pot_near, "band", [(i, i ^ 1) for i in range(groups)])
    bands = bands_in.reshape(LOCAL * HB, coefs)
    big_y, after_y = forward(bands, fwd_x, fwd_y)
    near_rows = near(near_at, after_y, pot_near, big_y, fwd_z)
    stepped_own, stepped_send = step(
        near_at, after_y, pot_far, big_y, fwd_z, near_rows, bands, back_x, send
    )
    received = exchange(stepped_send.reshape(groups, 2 * LOCAL, coefs // 2), "band")
    image_send = image(stepped_own, fwd_x_send)
    parts, stepped = gram(received.reshape(2 * NB, coefs // 2), image_send)
    parts = exchange(parts.reshape(groups, planes * LOCAL, -1), "band").reshape(2 * NB, -1)
    whole = exchange(total(parts).reshape(groups, LOCAL, NB), "band").reshape(NB, NB)
    phi, inverse = newton(whole, stepped)
    phi_local = exchange(phi.reshape(groups, 2 * LOCAL, coefs // 2), "band")
    pieces = density(patch_list, own, parts, inverse, big_y, fwd_z, hartree)
    pieces, phi_local = lax.optimization_barrier((pieces, phi_local))
    back = last(patch_list, own, exchange(pieces, "frag")).reshape(1, planes, FG * FG)
    bands_out = phi_local.reshape(groups, 2, LOCAL, coefs // 2).transpose(2, 0, 1, 3)
    bands_out = bands_out.astype(F32).reshape(1, LOCAL, HB * coefs)
    return (bands_out, back)


def solution(mesh):
    in_specs = (P("frag", "band", None), P("frag", "band", None), P("band", "frag", None), P())
    out_specs = (P("frag", "band", None), P("frag", "band", None))

    return jax.shard_map(
        per_device, mesh=mesh, in_specs=in_specs, out_specs=out_specs, check_vma=False
    )
```
